256 devices in a mesh: inst: 16 (over z_lo, x), section: 2 (over z_hi), tensor: 8 (over y, core).
Axes of the slice: x: 4, y: 4, z: 8 (z_hi: 2, z_lo: 4; z = z_hi * 4 + z_lo), core: 2. Of those that a mesh axis runs over, the one named last changes fastest.
Arguments:
- query_rows: bfloat16 [512, 4096], P('inst', 'tensor'), may hold values from -6 to 6
- new_kv: bfloat16 [512, 2, 1024], P('inst', None, 'tensor'), may hold values from -6 to 6
- residual: bfloat16 [512, 4096], P('inst', 'tensor'), may hold values from -6 to 6
- kv_cache: bfloat16 [2, 2048, 2, 128, 1024], P('section', 'inst', None, None, 'tensor'), may hold values from -6 to 6
- page_table: int32 [512, 4], P('inst'), may hold values from 0 to 127, as said below
- lengths: int32 [512], P('inst'), may hold values from 1 to 512, 131072 in all
- migrate_ids: int32 [128], P('inst'), may hold values from 0 to 31, as said below
- projection: bfloat16 [2, 4096, 4096], P('section', None, 'tensor')
- kv_weight: bfloat16 [4096, 2, 1024], P(None, None, 'tensor')
- norm_gain: float32 [4096], replicated, may hold values from 0.5 to 1.5
Outputs:
- attention_out: bfloat16 [2, 512, 4096], P('section', 'inst', 'tensor')
- hidden_out: bfloat16 [512, 4096], P('inst', 'tensor')
- migrated: bfloat16 [2, 128, 4, 2, 128, 1024], P('section', 'inst', None, None, None, 'tensor')
The draws below stay inside these ranges and needn't reach their ends.
Inputs may be any that keep to these rules, and one draw needn't show every extreme that they name: `page_table`: the 4 entries of a replica's 32 rows together name every page of its pool once. `migrate_ids`: the 8 ids of one replica are distinct requests of that replica.
All inputs are finite; a program needn't handle non-finite values. No bound on the sum of `lengths` on one device may be relied on, other than what follows from the above.
Results may differ from the reference program's by a relative error of at most 0.0065.
Values may be sent and summed in bfloat16 or wider, within the bound.
No kernel may reach another device: no remote copies, remote signals or barrier semaphores. Data moves between devices by JAX's collectives and lax.ppermute only.
A program may use at most 128 MiB of HBM per device.

```python
import math
import jax
import jax.numpy as jnp
import numpy as np
from jax import lax

D = 4096
HQ = 32
KVH = 8
HDIM = 128
PAGE = 128
PAGES_MAX = 4
REQ = 32
MIG = 8
POOL = 128
REQUESTS = 512
N_INST = 16


def table_orders(key):
    replica_keys = jax.random.split(jax.random.fold_in(key, 3), N_INST)

    def shuffle(item_key):
        return jax.random.permutation(item_key, POOL)
    return jax.vmap(shuffle)(replica_keys).astype(jnp.int32)


def draw_page_table(key, part):
    return table_orders(key).reshape(N_INST * REQ, PAGES_MAX).astype(jnp.int32)


def draw_migrate_ids(key, part):
    replica_keys = jax.random.split(jax.random.fold_in(key, 7), N_INST)

    def choose(item_key):
        return jax.random.permutation(item_key, REQ)[:MIG].astype(jnp.int32)
    drawn_rows = jax.vmap(choose)(replica_keys)
    chosen = jax.random.randint(jax.random.fold_in(key, 11), (), 0, N_INST)
    inner = 1 + jax.random.permutation(jax.random.fold_in(key, 13), REQ - 2)[:MIG - 2]
    special = jnp.concatenate([jnp.array([0, REQ - 1], jnp.int32), inner.astype(jnp.int32)])
    picked = (jnp.arange(N_INST) == chosen)[:, None]
    id_rows = jnp.where(picked, special[None, :], drawn_rows)
    return id_rows.reshape(N_INST * MIG).astype(jnp.int32)


def base_field(item_key, shape):
    return jnp.clip(jax.random.normal(item_key, shape, jnp.float32), -6.0, 6.0)


def align_plan(key):
    plan_key = jax.random.fold_in(key, 31)
    picked = jax.random.randint(jax.random.fold_in(plan_key, 1), (REQUESTS,), 0, 3) == 0
    forced = jax.random.randint(jax.random.fold_in(plan_key, 2), (), 0, REQUESTS)
    picked = picked | (jnp.arange(REQUESTS) == forced)
    heads = jax.random.randint(jax.random.fold_in(plan_key, 3), (REQUESTS,), 0, KVH)
    signs = (jax.random.randint(jax.random.fold_in(plan_key, 4), (REQUESTS, HDIM), 0, 2) * 2 - 1).astype(jnp.float32)
    key_size = jax.random.uniform(jax.random.fold_in(plan_key, 5), (REQUESTS,), jnp.float32, 4.0, 4.5)
    return (picked, heads, signs, key_size)


def draw_query_rows(key, part):
    picked, heads, signs, key_size = align_plan(key)
    base = base_field(jax.random.fold_in(key, 41), (REQUESTS, HQ * HDIM))
    group = HQ // KVH
    columns = jnp.arange(HQ * HDIM)
    query_head = columns // HDIM
    place = (query_head % group).astype(jnp.float32)
    strength = 5.5 - 3.0 * place / max(group - 1, 1)
    aligned = strength[None, :] * jnp.tile(signs, (1, HQ))
    chosen = picked[:, None] & ((query_head // group)[None, :] == heads[:, None])
    return jnp.where(chosen, aligned, base).astype(jnp.bfloat16)


def draw_new_kv(key, part):
    picked, heads, signs, key_size = align_plan(key)
    kv_width = KVH * HDIM
    base = base_field(jax.random.fold_in(key, 43), (REQUESTS, 2, kv_width))
    aligned = key_size[:, None] * jnp.tile(signs, (1, KVH))
    chosen = picked[:, None] & ((jnp.arange(kv_width) // HDIM)[None, :] == heads[:, None])
    fresh_keys = jnp.where(chosen, aligned, base[:, 0])
    return jnp.stack([fresh_keys, base[:, 1]], axis=1).astype(jnp.bfloat16)


def draw_kv_cache(key, part):
    picked, heads, signs, key_size = align_plan(key)
    owners = jnp.argsort(table_orders(key), axis=1) // PAGES_MAX
    cache_key = jax.random.fold_in(key, 51)
    kv_width = KVH * HDIM

    def replica(index):
        item_key = jax.random.fold_in(cache_key, index)
        base = base_field(item_key, (2, POOL, 2, PAGE, kv_width))
        rows = index * REQ + owners[index]
        shrink = jax.random.uniform(jax.random.fold_in(item_key, 1), (POOL, PAGE), jnp.float32, 0.008, 0.03)
        size_rows = key_size[rows][:, None] * (1.0 - shrink)
        direction = jnp.tile(signs[rows], (1, KVH))
        aligned = size_rows[:, :, None] * direction[:, None, :]
        chosen = picked[rows][:, None] & ((jnp.arange(kv_width) // HDIM)[None, :] == heads[rows][:, None])
        first_keys = jnp.where(chosen[:, None, :], aligned, base[0, :, 0])
        first_layer = jnp.stack([first_keys, base[0, :, 1]], axis=1)
        return jnp.stack([first_layer, base[1]], axis=0).astype(jnp.bfloat16)
    stacked = lax.map(replica, jnp.arange(N_INST))
    return jnp.transpose(stacked, (1, 0, 2, 3, 4, 5)).reshape(2, N_INST * POOL, 2, PAGE, kv_width)


def weight_plan(key):
    plan_key = jax.random.fold_in(key, 61)
    kv_base = base_field(jax.random.fold_in(plan_key, 1), (D, 2, KVH * HDIM)) * D ** (-0.5)
    picked = jax.random.randint(jax.random.fold_in(plan_key, 2), (HQ,), 0, 4) == 0
    forced = jax.random.randint(jax.random.fold_in(plan_key, 3), (), 0, HQ)
    picked = picked | (jnp.arange(HQ) == forced)
    strength = jax.random.uniform(jax.random.fold_in(plan_key, 4), (HQ,), jnp.float32, 10.0, 24.0)
    return (kv_base, picked, strength)


def draw_kv_weight(key, part):
    return weight_plan(key)[0].astype(jnp.bfloat16)


def draw_projection(key, part):
    kv_base, picked, strength = weight_plan(key)
    group = HQ // KVH
    out_proj = base_field(jax.random.fold_in(key, 71), (D, HQ * HDIM)) * D ** (-0.5)
    query_base = base_field(jax.random.fold_in(key, 72), (D, HQ * HDIM)) * D ** (-0.5)
    tied = jnp.repeat(kv_base[:, 0].reshape(D, KVH, HDIM), group, axis=1) * strength[None, :, None]
    tied = tied.reshape(D, HQ * HDIM)
    chosen = jnp.repeat(picked, HDIM)
    query_proj = jnp.where(chosen[None, :], tied, query_base)
    return jnp.stack([out_proj, query_proj]).astype(jnp.bfloat16)


def level_of(own_key, extent, pieces, low, high):
    def one(position, parts):
        heights = jax.random.uniform(jax.random.fold_in(jax.random.fold_in(own_key, 6), position), (parts,), jnp.float32, low / len(pieces), high / len(pieces))
        return jnp.repeat(jnp.exp(heights), extent[position] // parts).reshape((-1,) + (1,) * (len(extent) - position - 1))

    gain = one(*pieces[0])
    for cut in pieces[1:]:
        gain = gain * one(*cut)
    return gain


def length_profile(number_of, total, bound, skew):
    weights = [(1 << 20) // math.isqrt(grade ** skew) + 1 for grade in range(2, number_of + 1)]
    surplus, holding = total - bound - (number_of - 1), [1] * (number_of - 1)
    while surplus > 0:
        candidates = [i for i in range(number_of - 1) if holding[i] < bound]
        mass, remaining = sum([weights[i] for i in candidates]), surplus
        for i in candidates:
            more = min(bound - holding[i], max(1, remaining * weights[i] // mass), surplus)
            holding[i] = holding[i] + more
            surplus = surplus - more
    return np.array([bound] + holding)


def ragged(rng, number_of, total, limit, skew):
    if number_of == 2:
        one = jax.random.randint(rng, (), max(1, total - limit), min(limit, total - 1) + 1)
        return jnp.stack([one, total - one])
    tallies = jnp.asarray(length_profile(number_of, total, limit, skew), jnp.int32)
    couples = (number_of - 1) // 2
    giver, receiver = tallies[1:1 + 2 * couples:2], tallies[2:2 + 2 * couples:2]
    margin = jnp.minimum(giver - 1, limit - receiver)
    moved = jax.random.randint(jax.random.fold_in(rng, 1), (couples,), 0, 1 << 20) % (margin + 1)
    tallies = tallies.at[1:1 + 2 * couples:2].set(giver - moved).at[2:2 + 2 * couples:2].set(receiver + moved)
    return tallies[jax.random.permutation(jax.random.fold_in(rng, 2), number_of)]


def noise(key, extent, scale, bound, shards=(), kind=jnp.bfloat16):
    values = scale * jax.random.normal(key, extent, jnp.float32)
    if shards:
        values = values * level_of(key, extent, shards, -0.22, 0.18)
    return jnp.clip(values, -bound, bound).astype(kind)


def setup_inputs(seed: int = 0) -> dict:
    key_list = jax.random.split(jax.random.key(seed), 11)
    return {
        "query_rows": draw_query_rows(jax.random.fold_in(key_list[10], 71), 0),
        "new_kv": draw_new_kv(jax.random.fold_in(key_list[10], 71), 0),
        "residual": noise(key_list[2], (REQUESTS, D), 1.0, 6.0, ((0, 16), (1, 8))),
        "kv_cache": draw_kv_cache(jax.random.fold_in(key_list[10], 71), 0),
        "page_table": draw_page_table(jax.random.fold_in(key_list[10], 71), 0),
        "lengths": ragged(key_list[5], REQUESTS, REQUESTS * PAGES_MAX * PAGE // 2, PAGES_MAX * PAGE, 2).astype(jnp.int32),
        "migrate_ids": draw_migrate_ids(jax.random.fold_in(key_list[10], 71), 0),
        "projection": draw_projection(jax.random.fold_in(key_list[10], 71), 0),
        "kv_weight": draw_kv_weight(jax.random.fold_in(key_list[10], 71), 0),
        "norm_gain": jnp.clip(1.0 + 0.1 * jax.random.normal(key_list[9], (D,), jnp.float32), 0.5, 1.5),
    }


def attend(queries, fresh_rows, page_pool, table_rows, length_rows):
    count_rows = queries.shape[0]
    kv_width = page_pool.shape[-1]
    kv_heads = kv_width // HDIM
    group_size = queries.shape[1] // kv_width
    page_data = jnp.take(page_pool, table_rows, axis=0)
    span_len = page_data.shape[1] * page_data.shape[3]
    key_rows = page_data[:, :, 0].reshape(count_rows, span_len, kv_heads, HDIM).astype(jnp.float32)
    value_rows = page_data[:, :, 1].reshape(count_rows, span_len, kv_heads, HDIM).astype(jnp.float32)
    grouped = queries.reshape(count_rows, kv_heads, group_size, HDIM).astype(jnp.float32)
    score_scale = HDIM ** (-0.5)
    scores = jnp.einsum('nkgd,ntkd->nkgt', grouped, key_rows) * score_scale
    fresh_key = fresh_rows[:, 0].reshape(count_rows, kv_heads, HDIM).astype(jnp.float32)
    fresh_value = fresh_rows[:, 1].reshape(count_rows, kv_heads, 1, HDIM).astype(jnp.float32)
    fresh_score = jnp.einsum('nkgd,nkd->nkg', grouped, fresh_key) * score_scale
    positions = lax.broadcasted_iota(jnp.int32, (count_rows, span_len), 1)
    valid = positions < (length_rows - 1)[:, None]
    scores = jnp.where(valid[:, None, None, :], scores, jnp.float32(-1e+30))
    highest = jnp.maximum(lax.optimization_barrier(jnp.max(scores, axis=-1)), fresh_score)
    weights = jnp.exp(scores - highest[..., None])
    fresh_weight = jnp.exp(fresh_score - highest)
    denominator = lax.optimization_barrier(jnp.sum(weights, axis=-1)) + fresh_weight
    rounded = lax.optimization_barrier(weights.astype(jnp.bfloat16)).astype(jnp.float32)
    fresh_rounded = lax.optimization_barrier(fresh_weight.astype(jnp.bfloat16)).astype(jnp.float32)
    summed = jnp.einsum('nkgt,ntkd->nkgd', rounded, value_rows) + fresh_rounded[..., None] * fresh_value
    return (summed / denominator[..., None]).astype(jnp.bfloat16).reshape(count_rows, -1)

def gather_moved(page_pool, table_rows, length_rows, moved_ids):
    moved_table = jnp.take(table_rows, moved_ids, axis=0)
    moved_len = jnp.take(length_rows, moved_ids)
    page_data = jnp.take(page_pool, moved_table, axis=0)
    page_size = page_data.shape[3]
    page_used = lax.broadcasted_iota(jnp.int32, moved_table.shape, 1) * page_size < moved_len[:, None]
    kept = jnp.where(page_used[:, :, None, None, None], page_data, jnp.zeros_like(page_data))
    return (kept, moved_len)

def write_rows(kept, moved_len, moved_new):
    page_count = kept.shape[1]
    page_size = kept.shape[3]
    positions = lax.broadcasted_iota(jnp.int32, (page_count, page_size), 0) * page_size
    positions = positions + lax.broadcasted_iota(jnp.int32, (page_count, page_size), 1)
    write_mask = positions[None] == (moved_len - 1)[:, None, None]
    return jnp.where(write_mask[:, :, None, :, None], moved_new[:, None, :, None, :], kept)

def reference(query_rows, new_kv, residual, kv_cache, page_table, lengths, migrate_ids, projection, kv_weight, norm_gain):

    def replica(replica_index):
        row_start = (replica_index * REQ).astype(jnp.int32)
        queries = lax.dynamic_slice_in_dim(query_rows, row_start, REQ, 0)
        fresh_first = lax.dynamic_slice_in_dim(new_kv, row_start, REQ, 0)
        resid_rows = lax.dynamic_slice_in_dim(residual, row_start, REQ, 0)
        table_rows = lax.dynamic_slice_in_dim(page_table, row_start, REQ, 0)
        length_rows = lax.dynamic_slice_in_dim(lengths, row_start, REQ, 0)
        moved_ids = lax.dynamic_slice_in_dim(migrate_ids, (replica_index * MIG).astype(jnp.int32), MIG, 0)
        pools = lax.dynamic_slice_in_dim(kv_cache, (replica_index * POOL).astype(jnp.int32), POOL, 1)
        first_attn = attend(queries, fresh_first, pools[0], table_rows, length_rows)
        hidden = (resid_rows.astype(jnp.float32) + jnp.dot(first_attn, projection[0].T, preferred_element_type=jnp.float32)).astype(jnp.bfloat16)
        hidden_float = hidden.astype(jnp.float32)
        normed = (hidden_float * lax.rsqrt(lax.optimization_barrier(jnp.mean(hidden_float * hidden_float, axis=-1, keepdims=True)) + 1e-05) * norm_gain).astype(jnp.bfloat16)
        second_query = jnp.dot(normed, projection[1], preferred_element_type=jnp.float32).astype(jnp.bfloat16)
        second_kv = jnp.einsum('nd,dck->nck', normed.astype(jnp.float32), kv_weight.astype(jnp.float32)).astype(jnp.bfloat16)
        second_attn = attend(second_query, second_kv, pools[1], table_rows, length_rows)
        kept_first, moved_len = gather_moved(pools[0], table_rows, length_rows, moved_ids)
        kept_second, moved_len = gather_moved(pools[1], table_rows, length_rows, moved_ids)
        moved_first = write_rows(kept_first, moved_len, jnp.take(fresh_first, moved_ids, axis=0))
        moved_second = write_rows(kept_second, moved_len, jnp.take(second_kv, moved_ids, axis=0))
        return (first_attn, second_attn, hidden, jnp.stack([moved_first, moved_second]))
    first_all, second_all, hidden_all, moved_all = lax.map(replica, jnp.arange(N_INST, dtype=jnp.int32))
    attention_out = jnp.stack([first_all.reshape(REQUESTS, -1), second_all.reshape(REQUESTS, -1)])
    hidden_out = hidden_all.reshape(REQUESTS, -1)
    moved_all = jnp.roll(moved_all, 1, axis=0)
    moved_all = jnp.transpose(moved_all, (1, 0, 2, 3, 4, 5, 6))
    migrated = moved_all.reshape((2, N_INST * MIG) + moved_all.shape[3:])
    return (attention_out, hidden_out, migrated)
```

```python
import functools

import jax
import jax.numpy as jnp
from jax import lax
from jax.experimental import pallas as pl
from jax.experimental.pallas import tpu as pltpu
from jax.sharding import PartitionSpec as P

HDIM = 128
PAGE = 128
PAGES = 4
REQ = 32
MIG = 8
HEADS = 4
SPAN = PAGES * PAGE
WIDTH = HEADS * HDIM
D = 4096
ROWS = REQ + MIG
GROUP = 8
PAD = 8
SCALE = HDIM ** (-0.5)
F32 = jnp.float32
BF16 = jnp.bfloat16
ANY = pl.BlockSpec(memory_space=pl.ANY)
SMEM = pl.BlockSpec(memory_space=pltpu.SMEM)
VMEM = pl.BlockSpec(memory_space=pltpu.VMEM)


def leading():
    return lax.axis_index("section") == 0


def place():
    index = lax.axis_index("tensor")
    return index // 2, index % 2


def page_starts(table, pool, pages, sem):
    def start(r, _):
        for p in range(PAGES):
            pltpu.make_async_copy(
                pool.at[table[r, p]], pages.at[r, :, p], sem.at[r // GROUP]
            ).start()
        return 0

    lax.fori_loop(0, REQ, start, 0)


def attend(lengths, qs, ks, vs, os, pages, sem):
    lane = lax.broadcasted_iota(jnp.int32, (PAD, SPAN), 1)
    for g in range(REQ // GROUP):
        block = pages.at[pl.ds(g * GROUP, GROUP)]
        pltpu.make_async_copy(block, block, sem.at[g]).wait()
        rows = slice(g * GROUP * PAD, (g + 1) * GROUP * PAD)
        q = qs[rows, :]
        fresh = jnp.sum(q * ks[rows, :], axis=-1, keepdims=True) * SCALE
        scores = []
        for i in range(GROUP):
            r = g * GROUP + i
            keys = pages[r, 0].reshape(SPAN, HDIM)
            s = lax.dot_general(
                q[i * PAD : (i + 1) * PAD].astype(BF16),
                keys,
                (((1,), (1,)), ((), ())),
                preferred_element_type=F32,
            )
            scores.append(jnp.where(lane < lengths[r] - 1, s * SCALE, F32(-1e30)))
        s = jnp.concatenate(scores, axis=0)
        top = jnp.maximum(jnp.max(s, axis=-1, keepdims=True), fresh)
        w = jnp.exp(s - top)
        fw = jnp.exp(fresh - top)
        total = jnp.sum(w, axis=-1, keepdims=True) + fw
        outs = []
        for i in range(GROUP):
            r = g * GROUP + i
            values = pages[r, 1].reshape(SPAN, HDIM)
            outs.append(
                jnp.dot(
                    w[i * PAD : (i + 1) * PAD].astype(BF16),
                    values,
                    preferred_element_type=F32,
                )
            )
        o = jnp.concatenate(outs, axis=0) + fw.astype(BF16).astype(F32) * vs[rows, :]
        os[rows, :] = o / total


def spread(dst, h, value):
    dst[pl.ds(h, REQ, stride=PAD), :] = value.astype(F32)


def collect(os, out):
    for h in range(HEADS):
        out[:, h * HDIM : (h + 1) * HDIM] = os[pl.ds(h, REQ, stride=PAD), :].astype(BF16)


def gather_kernel(table, lengths, ids, pool, out, zero, sem):
    zero[...] = jnp.zeros_like(zero)

    def each(j, _):
        r = ids[j]
        for p in range(PAGES):
            used = p * PAGE < lengths[r]

            @pl.when(used)
            def _():
                pltpu.make_async_copy(pool.at[table[r, p]], out.at[j, p], sem).start()

            @pl.when(jnp.logical_not(used))
            def _():
                pltpu.make_async_copy(zero, out.at[j, p], sem).start()

        return 0

    lax.fori_loop(0, MIG, each, 0)
    pltpu.make_async_copy(out, out, sem).wait()


def gather_pages(table, lengths, ids, pool):
    return pl.pallas_call(
        gather_kernel,
        out_shape=jax.ShapeDtypeStruct((MIG, PAGES) + pool.shape[1:], BF16),
        in_specs=[SMEM, SMEM, SMEM, ANY],
        out_specs=ANY,
        scratch_shapes=[
            pltpu.VMEM(pool.shape[1:], BF16),
            pltpu.SemaphoreType.DMA,
        ],
        compiler_params=pltpu.CompilerParams(vmem_limit_bytes=4 << 20),
        name="gather_pages",
    )(table, lengths, ids, pool)


ATTEND_SCRATCH = [
    pltpu.VMEM((REQ, 2, PAGES, PAGE, HDIM), BF16),
    pltpu.VMEM((REQ * PAD, HDIM), F32),
    pltpu.VMEM((REQ * PAD, HDIM), F32),
    pltpu.VMEM((REQ * PAD, HDIM), F32),
    pltpu.VMEM((REQ * PAD, HDIM), F32),
    pltpu.SemaphoreType.DMA((REQ // GROUP,)),
]


def first_kernel(
    table, lengths, query, fresh_key, fresh_value, pool, weight, attn, keep, give,
    pages, qs, ks, vs, os, sem, held, wsem,
):
    y, core = place()

    @pl.when(leading())
    def _():
        page_starts(table, pool, pages, sem)
        copy = pltpu.make_async_copy(weight, held, wsem)
        copy.start()
        qs[...] = jnp.zeros_like(qs)
        ks[...] = jnp.zeros_like(ks)
        vs[...] = jnp.zeros_like(vs)
        for h in range(HEADS):
            spread(qs, h, query[:, h * HDIM : (h + 1) * HDIM])
            spread(ks, h, fresh_key[...])
            spread(vs, h, fresh_value[...])
        attend(lengths, qs, ks, vs, os, pages, sem)
        collect(os, attn)
        a = attn[...]
        copy.wait()
        for k in range(4):
            for out, c in ((give, 1 - core), (keep, core)):
                block = lax.rem(y + k, 4) * 2 + c
                w = held[pl.ds(pl.multiple_of(block * WIDTH, WIDTH), WIDTH), :]
                out[k] = lax.dot_general(
                    a, w, (((1,), (1,)), ((), ())), preferred_element_type=F32
                ).astype(out.dtype)

    @pl.when(jnp.logical_not(leading()))
    def _():
        attn[...] = jnp.zeros_like(attn)
        keep[...] = jnp.zeros_like(keep)
        give[...] = jnp.zeros_like(give)


def first_layer(table, lengths, query, fresh_key, fresh_value, pool, weight):
    part = (4, REQ, WIDTH)
    return pl.pallas_call(
        first_kernel,
        out_shape=(
            jax.ShapeDtypeStruct((REQ, WIDTH), BF16),
            jax.ShapeDtypeStruct(part, F32),
            jax.ShapeDtypeStruct(part, F32),
        ),
        in_specs=[SMEM, SMEM, VMEM, VMEM, VMEM, ANY, ANY],
        out_specs=(VMEM, VMEM, VMEM),
        scratch_shapes=ATTEND_SCRATCH
        + [pltpu.VMEM((D, WIDTH), BF16), pltpu.SemaphoreType.DMA],
        compiler_params=pltpu.CompilerParams(vmem_limit_bytes=24 << 20),
        name="first_layer",
    )(table, lengths, query, fresh_key, fresh_value, pool, weight)


def pair_kernel(keep, got, residual, own, a, b, c):
    own[...] = keep[0] + got[0] + residual[...].astype(F32)
    for k, out in ((1, a), (2, b), (3, c)):
        out[...] = (keep[k] + got[k]).astype(BF16)


def pair_sum(keep, got, residual):
    share = (REQ, WIDTH)
    return pl.pallas_call(
        pair_kernel,
        out_shape=(jax.ShapeDtypeStruct(share, F32),)
        + (jax.ShapeDtypeStruct(share, BF16),) * 3,
        in_specs=[VMEM] * 3,
        out_specs=(VMEM,) * 4,
        compiler_params=pltpu.CompilerParams(vmem_limit_bytes=4 << 20),
        name="pair_sum",
    )(keep, got, residual)


def share_kernel(ids, own, a, b, c, share, moved, wide):
    total = own[...] + a[...].astype(F32) + b[...].astype(F32) + c[...].astype(F32)
    rounded = total.astype(BF16)
    share[...] = rounded
    wide[...] = rounded.astype(F32)
    for j in range(MIG):
        moved[pl.ds(j, 1), :] = wide[pl.ds(ids[j], 1), :]


def share_sum(ids, own, a, b, c):
    return pl.pallas_call(
        share_kernel,
        out_shape=(
            jax.ShapeDtypeStruct((REQ, WIDTH), BF16),
            jax.ShapeDtypeStruct((MIG, WIDTH), F32),
        ),
        in_specs=[SMEM] + [VMEM] * 4,
        out_specs=(VMEM, VMEM),
        scratch_shapes=[pltpu.VMEM((REQ, WIDTH), F32)],
        compiler_params=pltpu.CompilerParams(vmem_limit_bytes=4 << 20),
        name="share_sum",
    )(ids, own, a, b, c)


def second_kernel(
    table, lengths, m0, m1, m2, m3, n0, n1, n2, n3, gain, pool, weight, kv_weight,
    attn, moved_kv,
    pages, qs, ks, vs, os, sem, held, wsem, held_kv, kvsem,
):
    y, core = place()

    @pl.when(jnp.logical_not(leading()))
    def _():
        wcopy = pltpu.make_async_copy(weight, held, wsem)
        wcopy.start()
        kvcopy = pltpu.make_async_copy(kv_weight, held_kv, kvsem)
        kvcopy.start()
        page_starts(table, pool, pages, sem)
        blocks = []
        square = jnp.zeros((ROWS, 1), F32)
        for refs, c in (((m0, m1, m2, m3), core), ((n0, n1, n2, n3), 1 - core)):
            for k, ref in enumerate(refs):
                x = ref[...].astype(F32)
                square += jnp.sum(x * x, axis=-1, keepdims=True)
                blocks.append((x, lax.rem(y + 4 - k, 4) * 2 + c))
        factor = lax.rsqrt(square * (1.0 / D) + 1e-05)
        wcopy.wait()
        kvcopy.wait()
        q = jnp.zeros((ROWS, WIDTH), F32)
        kv = jnp.zeros((ROWS, 2 * HDIM), F32)
        for x, block in blocks:
            x = (x * factor * gain[pl.ds(block, 1), :]).astype(BF16)
            at = pl.ds(pl.multiple_of(block * WIDTH, WIDTH), WIDTH)
            q += jnp.dot(x, held[at, :], preferred_element_type=F32)
            kv += jnp.dot(x, held_kv[at, :], preferred_element_type=F32)
        q = q.astype(BF16)
        kv = kv.astype(BF16).astype(F32)
        moved_kv[...] = kv[REQ:]
        qs[...] = jnp.zeros_like(qs)
        ks[...] = jnp.zeros_like(ks)
        vs[...] = jnp.zeros_like(vs)
        for h in range(HEADS):
            spread(qs, h, q[:REQ, h * HDIM : (h + 1) * HDIM])
            spread(ks, h, kv[:REQ, :HDIM])
            spread(vs, h, kv[:REQ, HDIM:])
        attend(lengths, qs, ks, vs, os, pages, sem)
        collect(os, attn)

    @pl.when(leading())
    def _():
        attn[...] = jnp.zeros_like(attn)
        moved_kv[...] = jnp.zeros_like(moved_kv)


def second_layer(table, lengths, mine, other, gain, pool, weight, kv_weight):
    return pl.pallas_call(
        second_kernel,
        out_shape=(
            jax.ShapeDtypeStruct((REQ, WIDTH), BF16),
            jax.ShapeDtypeStruct((MIG, 2 * HDIM), F32),
        ),
        in_specs=[SMEM, SMEM] + [VMEM] * 9 + [ANY] * 3,
        out_specs=(VMEM, VMEM),
        scratch_shapes=ATTEND_SCRATCH
        + [
            pltpu.VMEM((D, WIDTH), BF16),
            pltpu.SemaphoreType.DMA,
            pltpu.VMEM((D, 2 * HDIM), BF16),
            pltpu.SemaphoreType.DMA,
        ],
        compiler_params=pltpu.CompilerParams(vmem_limit_bytes=28 << 20),
        name="second_layer",
    )(table, lengths, *mine, *other, gain, pool, weight, kv_weight)


def patch_kernel(length, first_rows, second_rows, bulk, out, held, insem, outsem):
    for j in range(MIG):
        pltpu.make_async_copy(bulk.at[j], held.at[j], insem.at[j]).start()
    lead = leading()
    row = lax.broadcasted_iota(jnp.int32, (16, HDIM), 0)
    for j in range(MIG):
        pltpu.make_async_copy(bulk.at[j], held.at[j], insem.at[j]).wait()
        last = length[j] - 1
        page = last // PAGE
        base = pl.multiple_of((last % PAGE) // 16 * 16, 16)
        hit = row == last % 16
        for c in range(2):
            cols = slice(c * HDIM, (c + 1) * HDIM)
            new = jnp.where(lead, first_rows[pl.ds(j, 1), cols], second_rows[pl.ds(j, 1), cols])
            old = held[j, page, c, pl.ds(base, 16), :].astype(F32)
            held[j, page, c, pl.ds(base, 16), :] = jnp.where(hit, new, old).astype(BF16)
        pltpu.make_async_copy(held.at[j], out.at[j], outsem.at[j]).start()
    for j in range(MIG):
        pltpu.make_async_copy(held.at[j], out.at[j], outsem.at[j]).wait()


def patch(length, first_rows, second_rows, bulk):
    return pl.pallas_call(
        patch_kernel,
        out_shape=jax.ShapeDtypeStruct(bulk.shape, BF16),
        in_specs=[SMEM, VMEM, VMEM, ANY],
        out_specs=ANY,
        scratch_shapes=[
            pltpu.VMEM(bulk.shape, BF16),
            pltpu.SemaphoreType.DMA((MIG,)),
            pltpu.SemaphoreType.DMA((MIG,)),
        ],
        compiler_params=pltpu.CompilerParams(vmem_limit_bytes=8 << 20),
        name="patch",
    )(length, first_rows, second_rows, bulk)


def after(value, *others):
    return lax.optimization_barrier((value,) + others)[0]


def local(
    query_rows, new_kv, residual, kv_cache, page_table, lengths, migrate_ids,
    projection, kv_weight, norm_gain,
):
    replicas = lax.axis_size("inst")
    lead = leading()
    pool = kv_cache[0]
    weight = projection[0]

    def across(value, by):
        return lax.ppermute(value, "tensor", [(i, (i + 2 * by) % 8) for i in range(8)])

    def to_twin(value):
        return lax.ppermute(value, "tensor", [(i, i ^ 1) for i in range(8)])

    def to_next(value):
        return lax.ppermute(
            value, "inst", [(i, (i + 1) % replicas) for i in range(replicas)]
        )

    bulk = to_next(gather_pages(page_table, lengths, migrate_ids, pool))

    attn, keep, give = first_layer(
        page_table, lengths, query_rows, new_kv[:, 0], new_kv[:, 1], pool, weight
    )
    got = to_twin(give)
    own, a, b, c = pair_sum(keep, got, residual)
    share, moved = share_sum(migrate_ids, own, across(a, 1), across(b, 2), across(c, 3))
    moved = moved.astype(BF16)
    arrived = lax.ppermute(share, "section", [(0, 1)])
    moved_in = lax.ppermute(
        moved,
        ("inst", "section"),
        [(2 * i, 2 * ((i + 1) % replicas) + 1) for i in range(replicas)],
    )
    hidden = jnp.where(lead, share, arrived)

    ids = after(migrate_ids, moved)
    pick = (ids[:, None] == jnp.arange(REQ)[None, :]).astype(F32)
    side = jnp.concatenate(
        [new_kv.reshape(REQ, 2 * HDIM).astype(F32), jnp.broadcast_to(lengths.astype(F32)[:, None], (REQ, HDIM))],
        axis=1,
    )
    side = to_next(jnp.dot(pick, side, precision=lax.Precision.HIGHEST))
    first_rows = side[:, : 2 * HDIM]
    moved_len = side[:, 2 * HDIM].astype(jnp.int32)
    flat_kv = after(kv_weight, moved).reshape(D, 2 * HDIM)

    rows = jnp.concatenate([arrived, moved_in], axis=0)
    mine = [rows] + [across(rows, k) for k in (1, 2, 3)]
    other = [to_twin(m) for m in mine]
    second_attn, second_rows = second_layer(
        page_table, lengths, mine, other, norm_gain.reshape(8, WIDTH), pool, weight, flat_kv
    )
    migrated = patch(moved_len, first_rows, second_rows, bulk)
    attn = jnp.where(lead, attn, second_attn)
    return attn[None], hidden, migrated[None]


def solution(mesh):
    return jax.shard_map(
        local,
        mesh=mesh,
        in_specs=(
            P("inst", "tensor"),
            P("inst", None, "tensor"),
            P("inst", "tensor"),
            P("section", "inst", None, None, "tensor"),
            P("inst", None),
            P("inst"),
            P("inst"),
            P("section", None, "tensor"),
            P(None, None, "tensor"),
            P(),
        ),
        out_specs=(
            P("section", "inst", "tensor"),
            P("inst", "tensor"),
            P("section", "inst", None, None, None, "tensor"),
        ),
        check_vma=False,
    )
```

```python
import functools

import jax
import jax.numpy as jnp
from jax import lax
from jax.experimental import pallas as pl
from jax.experimental.pallas import tpu as pltpu
from jax.sharding import PartitionSpec as P

HDIM = 128
PAGE = 128
PAGES = 4
REQ = 32
MIG = 8
HEADS = 4
SPAN = PAGES * PAGE
WIDTH = HEADS * HDIM
D = 4096
POOL = 128
ROWS = REQ + MIG
SENT = 16
GROUP = 16
PAD = 8
PARTS = (8, 15, 9)
SCALE = HDIM ** (-0.5)
F32 = jnp.float32
BF16 = jnp.bfloat16
HBM = pl.BlockSpec(memory_space=pltpu.HBM)
VMEM = pl.BlockSpec(memory_space=pltpu.VMEM)
DMA = pltpu.SemaphoreType.DMA
KV = (2, PAGE, HDIM)


def in_hbm(*values):
    return [pltpu.with_memory_space_constraint(v, pltpu.HBM) for v in values]


def in_vmem(*values):
    return [pltpu.with_memory_space_constraint(v, pltpu.VMEM) for v in values]


def leading():
    return lax.axis_index("section") == 0


def place():
    index = lax.axis_index("tensor")
    return index // 2, index % 2


def started(*copies):
    made = [pltpu.make_async_copy(*c) for c in copies]
    for c in made:
        c.start()
    return made


def scores(lengths, table, qs, ks, pages, ss, g):
    lane = lax.broadcasted_iota(jnp.int32, (PAD, SPAN), 1)
    rows = slice(g * GROUP * PAD, (g + 1) * GROUP * PAD)
    q = qs[rows, :]
    for i in range(GROUP):
        r = g * GROUP + i
        own = q[i * PAD : (i + 1) * PAD].astype(BF16)
        s = jnp.concatenate(
            [
                lax.dot_general(
                    own,
                    pages[table[p, r], 0],
                    (((1,), (1,)), ((), ())),
                    preferred_element_type=F32,
                )
                for p in range(PAGES)
            ],
            axis=1,
        )
        ss[r * PAD : (r + 1) * PAD, :] = jnp.where(
            lane < lengths[r] - 1, s * SCALE, F32(-1e30)
        )


def mix(table, qs, ks, vs, os, pages, ss, g):
    rows = slice(g * GROUP * PAD, (g + 1) * GROUP * PAD)
    fresh = jnp.sum(qs[rows, :] * ks[rows, :], axis=-1, keepdims=True) * SCALE
    s = ss[rows, :]
    top = jnp.maximum(jnp.max(s, axis=-1, keepdims=True), fresh)
    w = jnp.exp(s - top)
    fw = jnp.exp(fresh - top)
    total = jnp.sum(w, axis=-1, keepdims=True) + fw
    outs = []
    for i in range(GROUP):
        r = g * GROUP + i
        rounded = w[i * PAD : (i + 1) * PAD].astype(BF16)
        values = jnp.concatenate([pages[table[p, r], 1] for p in range(PAGES)], axis=0)
        outs.append(jnp.dot(rounded, values, preferred_element_type=F32))
    o = jnp.concatenate(outs, axis=0) + fw.astype(BF16).astype(F32) * vs[rows, :]
    os[rows, :] = o / total


def spread(qs, ks, vs, q, k, v):
    for dst in (qs, ks, vs):
        dst[...] = jnp.zeros_like(dst)
    for h in range(HEADS):
        at = pl.ds(h, REQ, stride=PAD)
        qs[at, :] = q[:, h * HDIM : (h + 1) * HDIM]
        ks[at, :] = k
        vs[at, :] = v


def collect(os, out):
    for h in range(HEADS):
        out[:, h * HDIM : (h + 1) * HDIM] = os[pl.ds(h, REQ, stride=PAD), :].astype(BF16)


ROW_SCRATCH = [pltpu.VMEM((REQ * PAD, HDIM), F32)] * 4 + [pltpu.VMEM((REQ * PAD, SPAN), F32)]
TABLE_SCRATCH = [pltpu.SMEM((PAGES, REQ), jnp.int32), pltpu.SMEM((REQ,), jnp.int32)]


def write_row(ref, index, row, key, value):
    base = pl.multiple_of(row // 16 * 16, 16)
    hit = lax.broadcasted_iota(jnp.int32, (16, HDIM), 0) == row - base
    for c, new in ((0, key), (1, value)):
        old = ref[index, c, pl.ds(base, 16), :].astype(F32)
        ref[index, c, pl.ds(base, 16), :] = jnp.where(hit, new, old).astype(BF16)


def page_slots(refs):
    return [(ref, i) for ref, count in zip(refs, PARTS) for i in range(count)]


def gather_kernel(
    table_in, lengths_in, ids_in, fresh_in, pool, back, ahead, later,
    table, lengths, ids, fresh, small, sems,
):
    small_copies = started(
        (table_in, table, small.at[0]),
        (lengths_in, lengths, small.at[1]),
        (ids_in, ids, small.at[2]),
        (fresh_in, fresh, small.at[3]),
    )
    for c in small_copies[:3]:
        c.wait()
    slots = page_slots((back, ahead, later))

    def each(act):
        for j in range(MIG):
            r = ids[j]
            for p in range(PAGES):
                ref, index = slots[j * PAGES + p]
                act(r, p, ref.at[index], sems.at[j * PAGES + p])

    def start(r, p, slot, sem):
        used = p * PAGE < lengths[r]

        @pl.when(used)
        def _():
            pltpu.make_async_copy(pool.at[table[p, r]], slot, sem).start()

        @pl.when(jnp.logical_not(used))
        def _():
            slot[...] = jnp.zeros(KV, BF16)

    def wait(r, p, slot, sem):
        @pl.when(p * PAGE < lengths[r])
        def _():
            pltpu.make_async_copy(pool.at[0], slot, sem).wait()

    each(start)
    small_copies[3].wait()
    each(wait)

    @pl.when(leading())
    def _():
        for j in range(MIG):
            r = ids[j]
            last = lengths[r] - 1
            row = fresh[r].astype(F32)
            for p in range(PAGES):
                ref, index = slots[j * PAGES + p]

                @pl.when(last // PAGE == p)
                def _():
                    write_row(ref, index, last % PAGE, row[0:1], row[1:2])


def gather_pages(table, lengths, ids, fresh, pool):
    return pl.pallas_call(
        gather_kernel,
        out_shape=[jax.ShapeDtypeStruct((count,) + KV, BF16) for count in PARTS],
        in_specs=[HBM] * 5,
        out_specs=[VMEM] * 3,
        scratch_shapes=TABLE_SCRATCH
        + [
            pltpu.SMEM((MIG,), jnp.int32),
            pltpu.VMEM((REQ, 2, HDIM), BF16),
            DMA((4,)),
            DMA((MIG * PAGES,)),
        ],
        compiler_params=pltpu.CompilerParams(vmem_limit_bytes=4 << 20),
        name="gather_pages",
    )(*in_hbm(table, lengths, ids, fresh, pool))


def first_kernel(
    table_in, lengths_in, query_in, fresh_in, pages, weight_in,
    attn, keep, give, weight,
    qs, ks, vs, os, ss, table, lengths, query, fresh, small, wsem,
):
    y, core = place()
    lead = leading()
    [weight_copy] = started((weight_in, weight, wsem))

    @pl.when(lead)
    def _():
        copies = started(
            (table_in, table, small.at[0]),
            (lengths_in, lengths, small.at[1]),
            (query_in, query, small.at[2]),
            (fresh_in, fresh, small.at[3]),
        )
        for c in copies:
            c.wait()
        spread(
            qs, ks, vs,
            query[...].astype(F32), fresh[:, 0, :].astype(F32), fresh[:, 1, :].astype(F32),
        )
        for g in range(REQ // GROUP):
            scores(lengths, table, qs, ks, pages, ss, g)
        for g in range(REQ // GROUP):
            mix(table, qs, ks, vs, os, pages, ss, g)
        collect(os, attn)

    weight_copy.wait()

    @pl.when(lead)
    def _():
        a = attn[...]
        for out, c in ((give, 1 - core), (keep, core)):
            for k in range(4):
                block = lax.rem(y + k, 4) * 2 + c
                w = weight[pl.ds(pl.multiple_of(block * WIDTH, WIDTH), WIDTH), :]
                out[k] = lax.dot_general(
                    a, w, (((1,), (1,)), ((), ())), preferred_element_type=F32
                )

    @pl.when(jnp.logical_not(lead))
    def _():
        attn[...] = jnp.zeros_like(attn)
        keep[...] = jnp.zeros_like(keep)
        give[...] = jnp.zeros_like(give)


def first_layer(table, lengths, query, fresh, pages, weight):
    part = (4, REQ, WIDTH)
    return pl.pallas_call(
        first_kernel,
        out_shape=(
            jax.ShapeDtypeStruct((REQ, WIDTH), BF16),
            jax.ShapeDtypeStruct(part, F32),
            jax.ShapeDtypeStruct(part, F32),
            pltpu.VMEM((D, WIDTH), BF16),
        ),
        in_specs=[HBM] * 4 + [VMEM, HBM],
        out_specs=(VMEM,) * 4,
        scratch_shapes=ROW_SCRATCH
        + TABLE_SCRATCH
        + [
            pltpu.VMEM((REQ, WIDTH), BF16),
            pltpu.VMEM((REQ, 2, HDIM), BF16),
            DMA((4,)),
            DMA,
        ],
        compiler_params=pltpu.CompilerParams(vmem_limit_bytes=8 << 20),
        name="first_layer",
    )(*in_hbm(table, lengths, query, fresh), *in_vmem(pages), *in_hbm(weight))


def pair_kernel(keep, got, residual, own, a, b, c):
    own[...] = keep[0] + got[0] + residual[...].astype(F32)
    for k, out in ((1, a), (2, b), (3, c)):
        out[...] = (keep[k] + got[k]).astype(BF16)


def pair_sum(keep, got, residual):
    share = (REQ, WIDTH)
    return pl.pallas_call(
        pair_kernel,
        out_shape=(jax.ShapeDtypeStruct(share, F32),)
        + (jax.ShapeDtypeStruct(share, BF16),) * 3,
        in_specs=[VMEM] * 3,
        out_specs=(VMEM,) * 4,
        compiler_params=pltpu.CompilerParams(vmem_limit_bytes=4 << 20),
        name="pair_sum",
    )(keep, got, residual)


def share_kernel(ids_in, lengths_in, own, a, b, c, share, moved, wide, sent, ids, lengths, small):
    copies = started((ids_in, ids, small.at[0]), (lengths_in, lengths, small.at[1]))
    total = own[...] + a[...].astype(F32) + b[...].astype(F32) + c[...].astype(F32)
    rounded = total.astype(BF16)
    share[...] = rounded
    wide[...] = rounded.astype(F32)
    for copy in copies:
        copy.wait()
    lane = lax.broadcasted_iota(jnp.int32, (1, WIDTH), 1)
    for j in range(MIG):
        r = ids[j]
        sent[pl.ds(j, 1), :] = wide[pl.ds(r, 1), :]
        last = lengths[r] - 1
        sent[pl.ds(MIG + j, 1), :] = jnp.where(
            lane < HDIM, last // PAGE, last % PAGE
        ).astype(F32)
    moved[...] = sent[...].astype(BF16)


def share_sum(ids, lengths, own, a, b, c):
    return pl.pallas_call(
        share_kernel,
        out_shape=(
            jax.ShapeDtypeStruct((REQ, WIDTH), BF16),
            jax.ShapeDtypeStruct((SENT, WIDTH), BF16),
        ),
        in_specs=[HBM] * 2 + [VMEM] * 4,
        out_specs=(VMEM, VMEM),
        scratch_shapes=[
            pltpu.VMEM((REQ, WIDTH), F32),
            pltpu.VMEM((SENT, WIDTH), F32),
            pltpu.SMEM((MIG,), jnp.int32),
            pltpu.SMEM((REQ,), jnp.int32),
            DMA((2,)),
        ],
        compiler_params=pltpu.CompilerParams(vmem_limit_bytes=4 << 20),
        name="share_sum",
    )(*in_hbm(ids, lengths), own, a, b, c)


def join_kernel(share, arrived, moved_in, hidden, rows, last):
    lead = leading()

    @pl.when(lead)
    def _():
        hidden[...] = share[...]

    @pl.when(jnp.logical_not(lead))
    def _():
        hidden[...] = arrived[...]

    rows[:REQ, :] = arrived[...]
    rows[REQ:, :] = moved_in[:MIG, :]
    last[...] = moved_in[MIG:, : 2 * HDIM].astype(F32).astype(jnp.int32)


def join(share, arrived, moved_in):
    return pl.pallas_call(
        join_kernel,
        out_shape=(
            jax.ShapeDtypeStruct((REQ, WIDTH), BF16),
            jax.ShapeDtypeStruct((ROWS, WIDTH), BF16),
            jax.ShapeDtypeStruct((MIG, 2 * HDIM), jnp.int32),
        ),
        in_specs=[VMEM] * 3,
        out_specs=(VMEM,) * 3,
        compiler_params=pltpu.CompilerParams(vmem_limit_bytes=4 << 20),
        name="join",
    )(share, arrived, moved_in)


def second_kernel(
    table_in, lengths_in, first_attn, m0, m1, m2, m3, n0, n1, n2, n3, gain, pages, weight,
    kv_weight, attn, moved_kv,
    qs, ks, vs, os, ss, table, lengths, small,
):
    y, core = place()

    @pl.when(jnp.logical_not(leading()))
    def _():
        copies = started((table_in, table, small.at[0]), (lengths_in, lengths, small.at[1]))
        blocks = []
        square = jnp.zeros((ROWS, 1), F32)
        for refs, c in (((m0, m1, m2, m3), core), ((n0, n1, n2, n3), 1 - core)):
            for k, ref in enumerate(refs):
                x = ref[...].astype(F32)
                square += jnp.sum(x * x, axis=-1, keepdims=True)
                blocks.append((x, lax.rem(y + 4 - k, 4) * 2 + c))
        factor = lax.rsqrt(square * (1.0 / D) + 1e-05)
        q = jnp.zeros((ROWS, WIDTH), F32)
        kv = jnp.zeros((ROWS, 2 * HDIM), F32)
        for x, block in blocks:
            at = pl.ds(pl.multiple_of(block * WIDTH, WIDTH), WIDTH)
            x = (x * factor * gain[at].reshape(1, WIDTH)).astype(BF16)
            q += jnp.dot(x, weight[at, :], preferred_element_type=F32)
            kv += jnp.dot(x, kv_weight[at, :], preferred_element_type=F32)
        q = q.astype(BF16).astype(F32)
        kv = kv.astype(BF16).astype(F32)
        moved_kv[...] = kv[REQ:]
        spread(qs, ks, vs, q[:REQ], kv[:REQ, :HDIM], kv[:REQ, HDIM:])
        for copy in copies:
            copy.wait()
        for g in range(REQ // GROUP):
            scores(lengths, table, qs, ks, pages, ss, g)
        for g in range(REQ // GROUP):
            mix(table, qs, ks, vs, os, pages, ss, g)
        collect(os, attn)

    @pl.when(leading())
    def _():
        attn[...] = first_attn[...]
        moved_kv[...] = jnp.zeros_like(moved_kv)


def second_layer(table, lengths, first_attn, mine, other, gain, pages, weight, kv_weight):
    return pl.pallas_call(
        second_kernel,
        out_shape=(
            jax.ShapeDtypeStruct((REQ, WIDTH), BF16),
            jax.ShapeDtypeStruct((MIG, 2 * HDIM), F32),
        ),
        in_specs=[HBM] * 2 + [VMEM] * 13,
        out_specs=(VMEM, VMEM),
        scratch_shapes=ROW_SCRATCH + TABLE_SCRATCH + [DMA((2,))],
        compiler_params=pltpu.CompilerParams(vmem_limit_bytes=24 << 20),
        name="second_layer",
    )(*in_hbm(table, lengths), first_attn, *mine, *other, gain, *in_vmem(pages, weight, kv_weight))


def patch_kernel(last_in, rows, back, ahead, later, out, held, last, small, insem, outsem):
    [last_copy] = started((last_in, last, small))
    begin = [sum(PARTS[:i]) for i in range(3)]
    copies = started(
        *[
            (ref, held.at[pl.ds(begin[i], PARTS[i])], insem.at[i])
            for i, ref in enumerate((back, ahead, later))
        ]
    )
    last_copy.wait()
    for c in copies:
        c.wait()
    lead = leading()
    leave = []
    for j in range(MIG):

        @pl.when(jnp.logical_not(lead))
        def _():
            write_row(
                held,
                j * PAGES + last[j, 0],
                last[j, HDIM],
                rows[pl.ds(j, 1), :HDIM],
                rows[pl.ds(j, 1), HDIM:],
            )

        at = pl.ds(j * PAGES, PAGES)
        leave += started((held.at[at], out.at[at], outsem.at[j]))
    for c in leave:
        c.wait()


def patch(last, rows, *parts):
    shape = (MIG * PAGES,) + KV
    return pl.pallas_call(
        patch_kernel,
        out_shape=jax.ShapeDtypeStruct(shape, BF16),
        in_specs=[HBM, VMEM] + [pl.BlockSpec(memory_space=pl.ANY)] * 3,
        out_specs=HBM,
        scratch_shapes=[
            pltpu.VMEM(shape, BF16),
            pltpu.SMEM((MIG, 2 * HDIM), jnp.int32),
            DMA,
            DMA((3,)),
            DMA((MIG,)),
        ],
        compiler_params=pltpu.CompilerParams(vmem_limit_bytes=8 << 20),
        name="patch",
    )(last, rows, *parts)


def after(value, *others):
    return lax.optimization_barrier((value,) + others)[0]


def local(
    query_rows, new_kv, residual, kv_cache, page_table, lengths, migrate_ids,
    projection, kv_weight, norm_gain,
):
    replicas = lax.axis_size("inst")
    table = page_table.T

    def across(value, by):
        return lax.ppermute(value, "tensor", [(i, (i + 2 * by) % 8) for i in range(8)])

    def to_twin(value):
        return lax.ppermute(value, "tensor", [(i, i ^ 1) for i in range(8)])

    down = [(i, i // 4 * 4 + (i + 3) % 4) for i in range(replicas)]
    turn = [(i, (i + 3) % replicas) if i % 4 == 1 else pair for i, pair in enumerate(down)]

    def to_next(value):
        return lax.ppermute(
            value, "inst", [(i, (i + 1) % replicas) for i in range(replicas)]
        )

    pool = kv_cache[0]
    back, ahead, later = gather_pages(table, lengths, migrate_ids, new_kv, pool)
    ahead = to_next(ahead)
    back = lax.ppermute(back, "inst", down)

    attn, keep, give, weight = first_layer(
        table, lengths, query_rows, new_kv, pool, projection[0]
    )
    own, a, b, c = pair_sum(keep, to_twin(give), residual)
    share, moved = share_sum(
        migrate_ids, lengths, own, across(a, 1), across(b, 2), across(c, 3)
    )
    arrived = lax.ppermute(share, "section", [(0, 1), (1, 0)])
    links = [(2 * i, 2 * ((i + 1) % replicas) + 1) for i in range(replicas)]
    moved_in = lax.ppermute(
        moved, ("inst", "section"), links + [(b, a) for a, b in links]
    )
    flat_kv = after(kv_weight, share).reshape(D, 2 * HDIM)
    back = lax.ppermute(after(back, flat_kv), "inst", down)
    arrived = after(arrived, flat_kv)
    later = to_next(after(later, arrived, moved_in, ahead))

    hidden, rows, last = join(share, arrived, moved_in)
    mine = [rows] + [across(rows, k) for k in (1, 2, 3)]
    other = [to_twin(after(rows, mine[1]))] + [to_twin(m) for m in mine[1:]]
    back = lax.ppermute(after(back, rows), "inst", turn)
    attn, second_rows = second_layer(
        table, lengths, attn, mine, other, norm_gain, pool, weight, flat_kv
    )
    migrated = patch(last, second_rows, back, ahead, later)
    return attn[None], hidden, migrated.reshape((1, MIG, PAGES) + KV)


def solution(mesh):
    return jax.shard_map(
        local,
        mesh=mesh,
        in_specs=(
            P("inst", "tensor"),
            P("inst", None, "tensor"),
            P("inst", "tensor"),
            P("section", "inst", None, None, "tensor"),
            P("inst", None),
            P("inst"),
            P("inst"),
            P("section", None, "tensor"),
            P(None, None, "tensor"),
            P(),
        ),
        out_specs=(
            P("section", "inst", "tensor"),
            P("inst", "tensor"),
            P("section", "inst", None, None, None, "tensor"),
        ),
        check_vma=False,
    )
```

```python
import functools

import jax
import jax.numpy as jnp
from jax import lax
from jax.experimental import pallas as pl
from jax.experimental.pallas import tpu as pltpu
from jax.sharding import PartitionSpec as P

HDIM = 128
PAGE = 128
PAGES = 4
REQ = 32
MIG = 8
HEADS = 4
SPAN = PAGES * PAGE
WIDTH = HEADS * HDIM
D = 4096
POOL = 128
SENT = 2 * MIG
GROUP = 16
PAD = 8
PARTS = (6, 14, 12)
SCALE = HDIM ** (-0.5)
F32 = jnp.float32
BF16 = jnp.bfloat16
HBM = pl.BlockSpec(memory_space=pltpu.HBM)
VMEM = pl.BlockSpec(memory_space=pltpu.VMEM)
DMA = pltpu.SemaphoreType.DMA
KV = (2, PAGE, HDIM)


def in_hbm(*values):
    return [pltpu.with_memory_space_constraint(v, pltpu.HBM) for v in values]


def in_vmem(*values):
    return [pltpu.with_memory_space_constraint(v, pltpu.VMEM) for v in values]


def leading():
    return lax.axis_index("section") == 0


def place():
    index = lax.axis_index("tensor")
    return index // 2, index % 2


def started(*copies):
    made = [pltpu.make_async_copy(*c) for c in copies]
    for c in made:
        c.start()
    return made


def scores(lengths, table, qs, ks, pages, ss, g):
    lane = lax.broadcasted_iota(jnp.int32, (PAD, SPAN), 1)
    rows = slice(g * GROUP * PAD, (g + 1) * GROUP * PAD)
    q = qs[rows, :]
    for i in range(GROUP):
        r = g * GROUP + i
        own = q[i * PAD : (i + 1) * PAD].astype(BF16)
        s = jnp.concatenate(
            [
                lax.dot_general(
                    own,
                    pages[table[p, r], 0],
                    (((1,), (1,)), ((), ())),
                    preferred_element_type=F32,
                )
                for p in range(PAGES)
            ],
            axis=1,
        )
        ss[r * PAD : (r + 1) * PAD, :] = jnp.where(
            lane < lengths[r] - 1, s * SCALE, F32(-1e30)
        )


def mix(table, qs, ks, vs, os, pages, ss, g):
    rows = slice(g * GROUP * PAD, (g + 1) * GROUP * PAD)
    fresh = jnp.sum(qs[rows, :] * ks[rows, :], axis=-1, keepdims=True) * SCALE
    s = ss[rows, :]
    top = jnp.maximum(jnp.max(s, axis=-1, keepdims=True), fresh)
    w = jnp.exp(s - top)
    fw = jnp.exp(fresh - top)
    total = jnp.sum(w, axis=-1, keepdims=True) + fw
    outs = []
    for i in range(GROUP):
        r = g * GROUP + i
        rounded = w[i * PAD : (i + 1) * PAD].astype(BF16)
        values = jnp.concatenate([pages[table[p, r], 1] for p in range(PAGES)], axis=0)
        outs.append(jnp.dot(rounded, values, preferred_element_type=F32))
    o = jnp.concatenate(outs, axis=0) + fw.astype(BF16).astype(F32) * vs[rows, :]
    os[rows, :] = o / total


def spread(qs, ks, vs, q, k, v):
    for dst in (qs, ks, vs):
        dst[...] = jnp.zeros_like(dst)
    for h in range(HEADS):
        at = pl.ds(h, REQ, stride=PAD)
        qs[at, :] = q[:, h * HDIM : (h + 1) * HDIM]
        ks[at, :] = k
        vs[at, :] = v


def collect(os, out):
    for h in range(HEADS):
        out[:, h * HDIM : (h + 1) * HDIM] = os[pl.ds(h, REQ, stride=PAD), :].astype(BF16)


ROW_SCRATCH = [pltpu.VMEM((REQ * PAD, HDIM), F32)] * 4 + [pltpu.VMEM((REQ * PAD, SPAN), F32)]
TABLE_SCRATCH = [pltpu.SMEM((PAGES, REQ), jnp.int32), pltpu.SMEM((REQ,), jnp.int32)]


def write_row(ref, index, row, key, value):
    base = pl.multiple_of(row // 16 * 16, 16)
    hit = lax.broadcasted_iota(jnp.int32, (16, HDIM), 0) == row - base
    for c, new in ((0, key), (1, value)):
        old = ref[index, c, pl.ds(base, 16), :].astype(F32)
        ref[index, c, pl.ds(base, 16), :] = jnp.where(hit, new, old).astype(BF16)


def page_slots(refs):
    return [(ref, i) for ref, count in zip(refs, PARTS) for i in range(count)]


def gather_kernel(
    table_in, lengths_in, ids_in, fresh_in, pool, back, ahead, later,
    table, lengths, ids, fresh, small, sems,
):
    small_copies = started(
        (table_in, table, small.at[0]),
        (lengths_in, lengths, small.at[1]),
        (ids_in, ids, small.at[2]),
        (fresh_in, fresh, small.at[3]),
    )
    for c in small_copies[:3]:
        c.wait()
    slots = page_slots((back, ahead, later))

    def each(act):
        for j in range(MIG):
            r = ids[j]
            for p in range(PAGES):
                ref, index = slots[j * PAGES + p]
                act(r, p, ref.at[index], sems.at[j * PAGES + p])

    def start(r, p, slot, sem):
        used = p * PAGE < lengths[r]

        @pl.when(used)
        def _():
            pltpu.make_async_copy(pool.at[table[p, r]], slot, sem).start()

        @pl.when(jnp.logical_not(used))
        def _():
            slot[...] = jnp.zeros(KV, BF16)

    def wait(r, p, slot, sem):
        @pl.when(p * PAGE < lengths[r])
        def _():
            pltpu.make_async_copy(pool.at[0], slot, sem).wait()

    each(start)
    small_copies[3].wait()
    each(wait)

    @pl.when(leading())
    def _():
        for j in range(MIG):
            r = ids[j]
            last = lengths[r] - 1
            row = fresh[r].astype(F32)
            for p in range(PAGES):
                ref, index = slots[j * PAGES + p]

                @pl.when(last // PAGE == p)
                def _():
                    write_row(ref, index, last % PAGE, row[0:1], row[1:2])


def gather_pages(table, lengths, ids, fresh, pool):
    return pl.pallas_call(
        gather_kernel,
        out_shape=[jax.ShapeDtypeStruct((count,) + KV, BF16) for count in PARTS],
        in_specs=[HBM] * 5,
        out_specs=[VMEM] * 3,
        scratch_shapes=TABLE_SCRATCH
        + [
            pltpu.SMEM((MIG,), jnp.int32),
            pltpu.VMEM((REQ, 2, HDIM), BF16),
            DMA((4,)),
            DMA((MIG * PAGES,)),
        ],
        compiler_params=pltpu.CompilerParams(vmem_limit_bytes=4 << 20),
        name="gather_pages",
    )(*in_hbm(table, lengths, ids, fresh, pool))


def first_kernel(
    table_in, lengths_in, query_in, fresh_in, pages, weight_in,
    attn, keep, give, weight,
    qs, ks, vs, os, ss, table, lengths, query, fresh, small, wsem,
):
    y, core = place()
    lead = leading()
    [weight_copy] = started((weight_in, weight, wsem))

    @pl.when(lead)
    def _():
        copies = started(
            (table_in, table, small.at[0]),
            (lengths_in, lengths, small.at[1]),
            (query_in, query, small.at[2]),
            (fresh_in, fresh, small.at[3]),
        )
        for c in copies:
            c.wait()
        spread(
            qs, ks, vs,
            query[...].astype(F32), fresh[:, 0, :].astype(F32), fresh[:, 1, :].astype(F32),
        )
        for g in range(REQ // GROUP):
            scores(lengths, table, qs, ks, pages, ss, g)
        for g in range(REQ // GROUP):
            mix(table, qs, ks, vs, os, pages, ss, g)
        collect(os, attn)

    weight_copy.wait()

    @pl.when(lead)
    def _():
        a = attn[...]
        for out, c in ((give, 1 - core), (keep, core)):
            for k in range(4):
                block = lax.rem(y + k, 4) * 2 + c
                w = weight[pl.ds(pl.multiple_of(block * WIDTH, WIDTH), WIDTH), :]
                out[k] = lax.dot_general(
                    a, w, (((1,), (1,)), ((), ())), preferred_element_type=F32
                )

    @pl.when(jnp.logical_not(lead))
    def _():
        attn[...] = jnp.zeros_like(attn)
        keep[...] = jnp.zeros_like(keep)
        give[...] = jnp.zeros_like(give)


def first_layer(table, lengths, query, fresh, pages, weight):
    part = (4, REQ, WIDTH)
    return pl.pallas_call(
        first_kernel,
        out_shape=(
            jax.ShapeDtypeStruct((REQ, WIDTH), BF16),
            jax.ShapeDtypeStruct(part, F32),
            jax.ShapeDtypeStruct(part, F32),
            pltpu.VMEM((D, WIDTH), BF16),
        ),
        in_specs=[HBM] * 4 + [VMEM, HBM],
        out_specs=(VMEM,) * 4,
        scratch_shapes=ROW_SCRATCH
        + TABLE_SCRATCH
        + [
            pltpu.VMEM((REQ, WIDTH), BF16),
            pltpu.VMEM((REQ, 2, HDIM), BF16),
            DMA((4,)),
            DMA,
        ],
        compiler_params=pltpu.CompilerParams(vmem_limit_bytes=8 << 20),
        name="first_layer",
    )(*in_hbm(table, lengths, query, fresh), *in_vmem(pages), *in_hbm(weight))


def pair_kernel(keep, got, residual, own, a, b, c):
    own[...] = keep[0] + got[0] + residual[...].astype(F32)
    for k, out in ((1, a), (2, b), (3, c)):
        out[...] = (keep[k] + got[k]).astype(BF16)


def pair_sum(keep, got, residual):
    share = (REQ, WIDTH)
    return pl.pallas_call(
        pair_kernel,
        out_shape=(jax.ShapeDtypeStruct(share, F32),)
        + (jax.ShapeDtypeStruct(share, BF16),) * 3,
        in_specs=[VMEM] * 3,
        out_specs=(VMEM,) * 4,
        compiler_params=pltpu.CompilerParams(vmem_limit_bytes=4 << 20),
        name="pair_sum",
    )(keep, got, residual)


def share_kernel(own, a, b, c, share):
    total = own[...] + a[...].astype(F32) + b[...].astype(F32) + c[...].astype(F32)
    share[...] = total.astype(BF16)


def share_sum(own, a, b, c):
    return pl.pallas_call(
        share_kernel,
        out_shape=jax.ShapeDtypeStruct((REQ, WIDTH), BF16),
        in_specs=[VMEM] * 4,
        out_specs=VMEM,
        compiler_params=pltpu.CompilerParams(vmem_limit_bytes=4 << 20),
        name="share_sum",
    )(own, a, b, c)


def project_kernel(
    ids_in, lengths_in, share, m0, m1, m2, m3, n0, n1, n2, n3, gain, weight, kv_weight,
    hidden, query, fresh, moved,
    sent, ids, lengths, small,
):
    y, core = place()
    lead = leading()

    @pl.when(lead)
    def _():
        hidden[...] = share[...]
        query[...] = jnp.zeros_like(query)
        fresh[...] = jnp.zeros_like(fresh)
        moved[...] = jnp.zeros_like(moved)

    @pl.when(jnp.logical_not(lead))
    def _():
        copies = started((ids_in, ids, small.at[0]), (lengths_in, lengths, small.at[1]))
        hidden[...] = m0[...]
        blocks = []
        square = jnp.zeros((REQ, 1), F32)
        for refs, c in (((m0, m1, m2, m3), core), ((n0, n1, n2, n3), 1 - core)):
            for k, ref in enumerate(refs):
                x = ref[...].astype(F32)
                square += jnp.sum(x * x, axis=-1, keepdims=True)
                blocks.append((x, lax.rem(y + 4 - k, 4) * 2 + c))
        factor = lax.rsqrt(square * (1.0 / D) + 1e-05)
        q = jnp.zeros((REQ, WIDTH), F32)
        kv = jnp.zeros((REQ, 2 * HDIM), F32)
        for x, block in blocks:
            at = pl.ds(pl.multiple_of(block * WIDTH, WIDTH), WIDTH)
            x = (x * factor * gain[at].reshape(1, WIDTH)).astype(BF16)
            q += jnp.dot(x, weight[at, :], preferred_element_type=F32)
            kv += jnp.dot(x, kv_weight[at, :], preferred_element_type=F32)
        query[...] = q.astype(BF16)
        fresh[...] = kv.astype(BF16).astype(F32)
        for copy in copies:
            copy.wait()
        lane = lax.broadcasted_iota(jnp.int32, (1, 2 * HDIM), 1)
        for j in range(MIG):
            r = ids[j]
            sent[pl.ds(j, 1), :] = fresh[pl.ds(r, 1), :]
            last = lengths[r] - 1
            sent[pl.ds(MIG + j, 1), :] = jnp.where(
                lane < HDIM, last // PAGE, last % PAGE
            ).astype(F32)
        moved[...] = sent[...].astype(BF16)


def project(ids, lengths, share, mine, other, gain, weight, kv_weight):
    return pl.pallas_call(
        project_kernel,
        out_shape=(
            jax.ShapeDtypeStruct((REQ, WIDTH), BF16),
            jax.ShapeDtypeStruct((REQ, WIDTH), BF16),
            jax.ShapeDtypeStruct((REQ, 2 * HDIM), F32),
            jax.ShapeDtypeStruct((SENT, 2 * HDIM), BF16),
        ),
        in_specs=[HBM] * 2 + [VMEM] * 12,
        out_specs=(VMEM,) * 4,
        scratch_shapes=[
            pltpu.VMEM((SENT, 2 * HDIM), F32),
            pltpu.SMEM((MIG,), jnp.int32),
            pltpu.SMEM((REQ,), jnp.int32),
            DMA((2,)),
        ],
        compiler_params=pltpu.CompilerParams(vmem_limit_bytes=8 << 20),
        name="project",
    )(*in_hbm(ids, lengths), share, *mine, *other, gain, *in_vmem(weight, kv_weight))


def second_kernel(
    table_in, lengths_in, first_attn, query, fresh, pages, attn,
    qs, ks, vs, os, ss, table, lengths, small,
):
    @pl.when(jnp.logical_not(leading()))
    def _():
        copies = started((table_in, table, small.at[0]), (lengths_in, lengths, small.at[1]))
        spread(qs, ks, vs, query[...].astype(F32), fresh[:, :HDIM], fresh[:, HDIM:])
        for copy in copies:
            copy.wait()
        for g in range(REQ // GROUP):
            scores(lengths, table, qs, ks, pages, ss, g)
        for g in range(REQ // GROUP):
            mix(table, qs, ks, vs, os, pages, ss, g)
        collect(os, attn)

    @pl.when(leading())
    def _():
        attn[...] = first_attn[...]


def second_layer(table, lengths, first_attn, query, fresh, pages):
    return pl.pallas_call(
        second_kernel,
        out_shape=jax.ShapeDtypeStruct((REQ, WIDTH), BF16),
        in_specs=[HBM] * 2 + [VMEM] * 4,
        out_specs=VMEM,
        scratch_shapes=ROW_SCRATCH + TABLE_SCRATCH + [DMA((2,))],
        compiler_params=pltpu.CompilerParams(vmem_limit_bytes=8 << 20),
        cost_estimate=pl.CostEstimate(
            flops=1 << 30, bytes_accessed=16 << 20, transcendentals=1 << 20
        ),
        name="second_layer",
    )(*in_hbm(table, lengths), first_attn, query, fresh, *in_vmem(pages))


def patch_kernel(moved, back, ahead, soon, late, out, held, whole, last, rows, small, outsem):
    whole[...] = moved[MIG:, :].astype(F32).astype(jnp.int32)
    rows[...] = moved[:MIG, :].astype(F32)
    [last_copy] = started((whole, last, small))
    for i, (ref, index) in enumerate(page_slots((back, ahead))):
        held[i] = ref[index]
    turned = jnp.logical_and(leading(), lax.rem(lax.axis_index("inst"), 4) == 0)
    first = PARTS[0] + PARTS[1]

    @pl.when(turned)
    def _():
        for i in range(PARTS[2]):
            held[first + i] = late[i]

    @pl.when(jnp.logical_not(turned))
    def _():
        for i in range(PARTS[2]):
            held[first + i] = soon[i]

    last_copy.wait()
    lead = leading()
    leave = []
    for j in range(MIG):

        @pl.when(jnp.logical_not(lead))
        def _():
            write_row(
                held,
                j * PAGES + last[j, 0],
                last[j, HDIM],
                rows[pl.ds(j, 1), :HDIM],
                rows[pl.ds(j, 1), HDIM:],
            )

        at = pl.ds(j * PAGES, PAGES)
        leave += started((held.at[at], out.at[at], outsem.at[j]))
    for c in leave:
        c.wait()


def patch(moved, *parts):
    shape = (MIG * PAGES,) + KV
    return pl.pallas_call(
        patch_kernel,
        out_shape=jax.ShapeDtypeStruct(shape, BF16),
        in_specs=[VMEM] * 5,
        out_specs=HBM,
        scratch_shapes=[
            pltpu.VMEM(shape, BF16),
            pltpu.VMEM((MIG, 2 * HDIM), jnp.int32),
            pltpu.SMEM((MIG, 2 * HDIM), jnp.int32),
            pltpu.VMEM((MIG, 2 * HDIM), F32),
            DMA,
            DMA((MIG,)),
        ],
        compiler_params=pltpu.CompilerParams(vmem_limit_bytes=8 << 20),
        name="patch",
    )(moved, *parts)


def after(value, *others):
    return lax.optimization_barrier((value,) + others)[0]


def local(
    query_rows, new_kv, residual, kv_cache, page_table, lengths, migrate_ids,
    projection, kv_weight, norm_gain,
):
    replicas = lax.axis_size("inst")
    table = page_table.T

    def across(value, by):
        return lax.ppermute(value, "tensor", [(i, (i + 2 * by) % 8) for i in range(8)])

    def to_twin(value):
        return lax.ppermute(value, "tensor", [(i, i ^ 1) for i in range(8)])

    down = [(i, i // 4 * 4 + (i + 3) % 4) for i in range(replicas)]
    turn = [(i, (i + 3) % replicas) if i % 4 == 1 else pair for i, pair in enumerate(down)]

    def to_next(value):
        return lax.ppermute(
            value, "inst", [(i, (i + 1) % replicas) for i in range(replicas)]
        )

    pool = kv_cache[0]
    back, ahead, later = gather_pages(table, lengths, migrate_ids, new_kv, pool)
    ahead = to_next(ahead)
    back = lax.ppermute(back, "inst", down)

    attn, keep, give, weight = first_layer(
        table, lengths, query_rows, new_kv, pool, projection[0]
    )
    own, a, b, c = pair_sum(keep, to_twin(give), residual)
    share = share_sum(own, across(a, 1), across(b, 2), across(c, 3))
    across_z = [(2 * i, 2 * i + 1) for i in range(replicas)]
    across_z += [(b, a) for a, b in across_z if a % 8 != 6]
    arrived = lax.ppermute(share, ("inst", "section"), across_z)
    back = lax.ppermute(after(back, share), "inst", down)
    flat_kv = after(kv_weight, share).reshape(D, 2 * HDIM)
    steps = [
        (2 * i + k, 2 * ((i + 1) % replicas) + k) for i in range(replicas) for k in range(2)
    ]
    turns = [(a, b) for a, b in steps if a % 8 == 6]
    later = after(later, share)
    soon = lax.ppermute(later, ("inst", "section"), [p for p in steps if p not in turns])
    arrived = after(arrived, flat_kv, ahead)
    late = lax.ppermute(after(later, arrived), ("inst", "section"), turns)

    mine = [arrived] + [across(arrived, k) for k in (1, 2, 3)]
    other = [to_twin(after(arrived, mine[1]))] + [to_twin(m) for m in mine[1:]]
    back = lax.ppermute(after(back, *mine), "inst", turn)
    hidden, query, fresh, moved = project(
        migrate_ids, lengths, share, mine, other, norm_gain, weight, flat_kv
    )
    moved = lax.ppermute(
        moved,
        ("inst", "section"),
        [(2 * i + 1, 2 * ((i + 1) % replicas) + 1) for i in range(replicas)],
    )
    attn = second_layer(table, lengths, attn, query, fresh, pool)
    migrated = patch(moved, back, ahead, soon, late)
    return attn[None], hidden, migrated.reshape((1, MIG, PAGES) + KV)


def solution(mesh):
    return jax.shard_map(
        local,
        mesh=mesh,
        in_specs=(
            P("inst", "tensor"),
            P("inst", None, "tensor"),
            P("inst", "tensor"),
            P("section", "inst", None, None, "tensor"),
            P("inst", None),
            P("inst"),
            P("inst"),
            P("section", None, "tensor"),
            P(None, None, "tensor"),
            P(),
        ),
        out_specs=(
            P("section", "inst", "tensor"),
            P("inst", "tensor"),
            P("section", "inst", None, None, None, "tensor"),
        ),
        check_vma=False,
    )
```

```python
import functools

import jax
import jax.numpy as jnp
from jax import lax
from jax.experimental import pallas as pl
from jax.experimental.pallas import tpu as pltpu
from jax.sharding import PartitionSpec as P

HDIM = 128
PAGE = 128
PAGES = 4
REQ = 32
MIG = 8
HEADS = 4
SPAN = PAGES * PAGE
WIDTH = HEADS * HDIM
D = 4096
POOL = 128
SENT = 2 * MIG
GROUP = 16
PAD = 8
PARTS = (6, 14, 12)
SCALE = HDIM ** (-0.5)
F32 = jnp.float32
BF16 = jnp.bfloat16
HBM = pl.BlockSpec(memory_space=pltpu.HBM)
VMEM = pl.BlockSpec(memory_space=pltpu.VMEM)
DMA = pltpu.SemaphoreType.DMA
KV = (2, PAGE, HDIM)


def in_hbm(*values):
    return [pltpu.with_memory_space_constraint(v, pltpu.HBM) for v in values]


def in_vmem(*values):
    return [pltpu.with_memory_space_constraint(v, pltpu.VMEM) for v in values]


def leading():
    return lax.axis_index("section") == 0


def place():
    index = lax.axis_index("tensor")
    return index // 2, index % 2


def started(*copies):
    made = [pltpu.make_async_copy(*c) for c in copies]
    for c in made:
        c.start()
    return made


def scores(lengths, table, qs, ks, pages, ss, g):
    lane = lax.broadcasted_iota(jnp.int32, (PAD, SPAN), 1)
    rows = slice(g * GROUP * PAD, (g + 1) * GROUP * PAD)
    q = qs[rows, :]
    for i in range(GROUP):
        r = g * GROUP + i
        own = q[i * PAD : (i + 1) * PAD].astype(BF16)
        s = jnp.concatenate(
            [
                lax.dot_general(
                    own,
                    pages[table[p, r], 0],
                    (((1,), (1,)), ((), ())),
                    preferred_element_type=F32,
                )
                for p in range(PAGES)
            ],
            axis=1,
        )
        ss[r * PAD : (r + 1) * PAD, :] = jnp.where(
            lane < lengths[r] - 1, s * SCALE, F32(-1e30)
        )


def mix(table, qs, ks, vs, os, pages, ss, g):
    rows = slice(g * GROUP * PAD, (g + 1) * GROUP * PAD)
    fresh = jnp.sum(qs[rows, :] * ks[rows, :], axis=-1, keepdims=True) * SCALE
    s = ss[rows, :]
    top = jnp.maximum(jnp.max(s, axis=-1, keepdims=True), fresh)
    w = jnp.exp(s - top)
    fw = jnp.exp(fresh - top)
    total = jnp.sum(w, axis=-1, keepdims=True) + fw
    outs = []
    for i in range(GROUP):
        r = g * GROUP + i
        rounded = w[i * PAD : (i + 1) * PAD].astype(BF16)
        values = jnp.concatenate([pages[table[p, r], 1] for p in range(PAGES)], axis=0)
        outs.append(jnp.dot(rounded, values, preferred_element_type=F32))
    o = jnp.concatenate(outs, axis=0) + fw.astype(BF16).astype(F32) * vs[rows, :]
    os[rows, :] = o / total


def spread(qs, ks, vs, q, k, v):
    for dst in (qs, ks, vs):
        dst[...] = jnp.zeros_like(dst)
    for h in range(HEADS):
        at = pl.ds(h, REQ, stride=PAD)
        qs[at, :] = q[:, h * HDIM : (h + 1) * HDIM]
        ks[at, :] = k
        vs[at, :] = v


def collect(os, out):
    for h in range(HEADS):
        out[:, h * HDIM : (h + 1) * HDIM] = os[pl.ds(h, REQ, stride=PAD), :].astype(BF16)


ROW_SCRATCH = [pltpu.VMEM((REQ * PAD, HDIM), F32)] * 4 + [pltpu.VMEM((REQ * PAD, SPAN), F32)]
TABLE_SCRATCH = [pltpu.SMEM((PAGES, REQ), jnp.int32), pltpu.SMEM((REQ,), jnp.int32)]


def write_row(ref, index, row, key, value):
    base = pl.multiple_of(row // 16 * 16, 16)
    hit = lax.broadcasted_iota(jnp.int32, (16, HDIM), 0) == row - base
    for c, new in ((0, key), (1, value)):
        old = ref[index, c, pl.ds(base, 16), :].astype(F32)
        ref[index, c, pl.ds(base, 16), :] = jnp.where(hit, new, old).astype(BF16)


def page_slots(refs):
    return [(ref, i) for ref, count in zip(refs, PARTS) for i in range(count)]


def gather_kernel(
    table_in, lengths_in, ids_in, fresh_in, pool, back, ahead, later,
    table, lengths, ids, fresh, small, sems,
):
    small_copies = started(
        (table_in, table, small.at[0]),
        (lengths_in, lengths, small.at[1]),
        (ids_in, ids, small.at[2]),
        (fresh_in, fresh, small.at[3]),
    )
    for c in small_copies[:3]:
        c.wait()
    slots = page_slots((back, ahead, later))

    def each(act):
        for j in range(MIG):
            r = ids[j]
            for p in range(PAGES):
                ref, index = slots[j * PAGES + p]
                act(r, p, ref.at[index], sems.at[j * PAGES + p])

    def start(r, p, slot, sem):
        used = p * PAGE < lengths[r]

        @pl.when(used)
        def _():
            pltpu.make_async_copy(pool.at[table[p, r]], slot, sem).start()

        @pl.when(jnp.logical_not(used))
        def _():
            slot[...] = jnp.zeros(KV, BF16)

    def wait(r, p, slot, sem):
        @pl.when(p * PAGE < lengths[r])
        def _():
            pltpu.make_async_copy(pool.at[0], slot, sem).wait()

    each(start)
    small_copies[3].wait()
    each(wait)

    @pl.when(leading())
    def _():
        for j in range(MIG):
            r = ids[j]
            last = lengths[r] - 1
            row = fresh[r].astype(F32)
            for p in range(PAGES):
                ref, index = slots[j * PAGES + p]

                @pl.when(last // PAGE == p)
                def _():
                    write_row(ref, index, last % PAGE, row[0:1], row[1:2])


def gather_pages(table, lengths, ids, fresh, pool):
    return pl.pallas_call(
        gather_kernel,
        out_shape=[jax.ShapeDtypeStruct((count,) + KV, BF16) for count in PARTS],
        in_specs=[HBM] * 5,
        out_specs=[VMEM] * 3,
        scratch_shapes=TABLE_SCRATCH
        + [
            pltpu.SMEM((MIG,), jnp.int32),
            pltpu.VMEM((REQ, 2, HDIM), BF16),
            DMA((4,)),
            DMA((MIG * PAGES,)),
        ],
        compiler_params=pltpu.CompilerParams(vmem_limit_bytes=4 << 20),
        name="gather_pages",
    )(*in_hbm(table, lengths, ids, fresh, pool))


def first_kernel(
    table_in, lengths_in, query_in, fresh_in, pages, weight_in,
    attn, keep, give, weight,
    qs, ks, vs, os, ss, table, lengths, query, fresh, small, wsem,
):
    y, core = place()
    lead = leading()
    [weight_copy] = started((weight_in, weight, wsem))

    @pl.when(lead)
    def _():
        copies = started(
            (table_in, table, small.at[0]),
            (lengths_in, lengths, small.at[1]),
            (query_in, query, small.at[2]),
            (fresh_in, fresh, small.at[3]),
        )
        for c in copies:
            c.wait()
        spread(
            qs, ks, vs,
            query[...].astype(F32), fresh[:, 0, :].astype(F32), fresh[:, 1, :].astype(F32),
        )
        for g in range(REQ // GROUP):
            scores(lengths, table, qs, ks, pages, ss, g)
        for g in range(REQ // GROUP):
            mix(table, qs, ks, vs, os, pages, ss, g)
        collect(os, attn)

    weight_copy.wait()

    @pl.when(lead)
    def _():
        a = attn[...]
        for out, c in ((give, 1 - core), (keep, core)):
            for k in range(4):
                block = lax.rem(y + k, 4) * 2 + c
                w = weight[pl.ds(pl.multiple_of(block * WIDTH, WIDTH), WIDTH), :]
                out[k] = lax.dot_general(
                    a, w, (((1,), (1,)), ((), ())), preferred_element_type=F32
                )

    @pl.when(jnp.logical_not(lead))
    def _():
        attn[...] = jnp.zeros_like(attn)
        keep[...] = jnp.zeros_like(keep)
        give[...] = jnp.zeros_like(give)


def first_layer(table, lengths, query, fresh, pages, weight):
    part = (4, REQ, WIDTH)
    return pl.pallas_call(
        first_kernel,
        out_shape=(
            jax.ShapeDtypeStruct((REQ, WIDTH), BF16),
            jax.ShapeDtypeStruct(part, F32),
            jax.ShapeDtypeStruct(part, F32),
            pltpu.VMEM((D, WIDTH), BF16),
        ),
        in_specs=[HBM] * 4 + [VMEM, HBM],
        out_specs=(VMEM,) * 4,
        scratch_shapes=ROW_SCRATCH
        + TABLE_SCRATCH
        + [
            pltpu.VMEM((REQ, WIDTH), BF16),
            pltpu.VMEM((REQ, 2, HDIM), BF16),
            DMA((4,)),
            DMA,
        ],
        compiler_params=pltpu.CompilerParams(vmem_limit_bytes=8 << 20),
        name="first_layer",
    )(*in_hbm(table, lengths, query, fresh), *in_vmem(pages), *in_hbm(weight))


def pair_kernel(keep, got, residual, own, a, b, c):
    own[...] = keep[0] + got[0] + residual[...].astype(F32)
    for k, out in ((1, a), (2, b), (3, c)):
        out[...] = (keep[k] + got[k]).astype(BF16)


def pair_sum(keep, got, residual):
    share = (REQ, WIDTH)
    return pl.pallas_call(
        pair_kernel,
        out_shape=(jax.ShapeDtypeStruct(share, F32),)
        + (jax.ShapeDtypeStruct(share, BF16),) * 3,
        in_specs=[VMEM] * 3,
        out_specs=(VMEM,) * 4,
        compiler_params=pltpu.CompilerParams(vmem_limit_bytes=4 << 20),
        name="pair_sum",
    )(keep, got, residual)


def share_kernel(own, a, b, c, share):
    total = own[...] + a[...].astype(F32) + b[...].astype(F32) + c[...].astype(F32)
    share[...] = total.astype(BF16)


def share_sum(own, a, b, c):
    return pl.pallas_call(
        share_kernel,
        out_shape=jax.ShapeDtypeStruct((REQ, WIDTH), BF16),
        in_specs=[VMEM] * 4,
        out_specs=VMEM,
        compiler_params=pltpu.CompilerParams(vmem_limit_bytes=4 << 20),
        name="share_sum",
    )(own, a, b, c)


def project_kernel(
    ids_in, lengths_in, share, m0, m1, m2, m3, n0, n1, n2, n3, gain, weight, kv_weight,
    hidden, query, fresh, moved,
    sent, ids, lengths, small,
):
    y, core = place()
    lead = leading()

    @pl.when(lead)
    def _():
        hidden[...] = share[...]
        query[...] = jnp.zeros_like(query)
        fresh[...] = jnp.zeros_like(fresh)
        moved[...] = jnp.zeros_like(moved)

    @pl.when(jnp.logical_not(lead))
    def _():
        copies = started((ids_in, ids, small.at[0]), (lengths_in, lengths, small.at[1]))
        hidden[...] = m0[...]
        blocks = []
        square = jnp.zeros((REQ, 1), F32)
        for refs, c in (((m0, m1, m2, m3), core), ((n0, n1, n2, n3), 1 - core)):
            for k, ref in enumerate(refs):
                x = ref[...].astype(F32)
                square += jnp.sum(x * x, axis=-1, keepdims=True)
                blocks.append((x, lax.rem(y + 4 - k, 4) * 2 + c))
        factor = lax.rsqrt(square * (1.0 / D) + 1e-05)
        q = jnp.zeros((REQ, WIDTH), F32)
        kv = jnp.zeros((REQ, 2 * HDIM), F32)
        for x, block in blocks:
            at = pl.ds(pl.multiple_of(block * WIDTH, WIDTH), WIDTH)
            x = (x * factor * gain[at].reshape(1, WIDTH)).astype(BF16)
            q += jnp.dot(x, weight[at, :], preferred_element_type=F32)
            kv += jnp.dot(x, kv_weight[at, :], preferred_element_type=F32)
        query[...] = q.astype(BF16)
        fresh[...] = kv.astype(BF16).astype(F32)
        for copy in copies:
            copy.wait()
        lane = lax.broadcasted_iota(jnp.int32, (1, 2 * HDIM), 1)
        for j in range(MIG):
            r = ids[j]
            sent[pl.ds(j, 1), :] = fresh[pl.ds(r, 1), :]
            last = lengths[r] - 1
            sent[pl.ds(MIG + j, 1), :] = jnp.where(
                lane < HDIM, last // PAGE, last % PAGE
            ).astype(F32)
        moved[...] = sent[...].astype(BF16)


def project(ids, lengths, share, mine, other, gain, weight, kv_weight):
    return pl.pallas_call(
        project_kernel,
        out_shape=(
            jax.ShapeDtypeStruct((REQ, WIDTH), BF16),
            jax.ShapeDtypeStruct((REQ, WIDTH), BF16),
            jax.ShapeDtypeStruct((REQ, 2 * HDIM), F32),
            jax.ShapeDtypeStruct((SENT, 2 * HDIM), BF16),
        ),
        in_specs=[HBM] * 2 + [VMEM] * 12,
        out_specs=(VMEM,) * 4,
        scratch_shapes=[
            pltpu.VMEM((SENT, 2 * HDIM), F32),
            pltpu.SMEM((MIG,), jnp.int32),
            pltpu.SMEM((REQ,), jnp.int32),
            DMA((2,)),
        ],
        compiler_params=pltpu.CompilerParams(vmem_limit_bytes=8 << 20),
        name="project",
    )(*in_hbm(ids, lengths), share, *mine, *other, gain, *in_vmem(weight, kv_weight))


def second_kernel(
    table_in, lengths_in, first_attn, query, fresh, pages, attn,
    qs, ks, vs, os, ss, table, lengths, small,
):
    @pl.when(jnp.logical_not(leading()))
    def _():
        copies = started((table_in, table, small.at[0]), (lengths_in, lengths, small.at[1]))
        spread(qs, ks, vs, query[...].astype(F32), fresh[:, :HDIM], fresh[:, HDIM:])
        for copy in copies:
            copy.wait()
        for g in range(REQ // GROUP):
            scores(lengths, table, qs, ks, pages, ss, g)
        for g in range(REQ // GROUP):
            mix(table, qs, ks, vs, os, pages, ss, g)
        collect(os, attn)

    @pl.when(leading())
    def _():
        attn[...] = first_attn[...]


def second_layer(table, lengths, first_attn, query, fresh, pages):
    return pl.pallas_call(
        second_kernel,
        out_shape=jax.ShapeDtypeStruct((REQ, WIDTH), BF16),
        in_specs=[HBM] * 2 + [VMEM] * 4,
        out_specs=VMEM,
        scratch_shapes=ROW_SCRATCH + TABLE_SCRATCH + [DMA((2,))],
        compiler_params=pltpu.CompilerParams(vmem_limit_bytes=8 << 20),
        cost_estimate=pl.CostEstimate(
            flops=1 << 30, bytes_accessed=16 << 20, transcendentals=1 << 20
        ),
        name="second_layer",
    )(*in_hbm(table, lengths), first_attn, query, fresh, *in_vmem(pages))


def patch_kernel(moved, back, ahead, soon, late, out, held, whole, last, rows, small, outsem):
    whole[...] = moved[MIG:, :].astype(F32).astype(jnp.int32)
    rows[...] = moved[:MIG, :].astype(F32)
    [last_copy] = started((whole, last, small))
    for i, (ref, index) in enumerate(page_slots((back, ahead))):
        held[i] = ref[index]
    turned = jnp.logical_and(leading(), lax.rem(lax.axis_index("inst"), 4) == 0)
    first = PARTS[0] + PARTS[1]

    @pl.when(turned)
    def _():
        for i in range(PARTS[2]):
            held[first + i] = late[i]

    @pl.when(jnp.logical_not(turned))
    def _():
        for i in range(PARTS[2]):
            held[first + i] = soon[i]

    last_copy.wait()
    lead = leading()
    leave = []
    for j in range(MIG):

        @pl.when(jnp.logical_not(lead))
        def _():
            write_row(
                held,
                j * PAGES + last[j, 0],
                last[j, HDIM],
                rows[pl.ds(j, 1), :HDIM],
                rows[pl.ds(j, 1), HDIM:],
            )

        at = pl.ds(j * PAGES, PAGES)
        leave += started((held.at[at], out.at[at], outsem.at[j]))
    for c in leave:
        c.wait()


def patch(moved, *parts):
    shape = (MIG * PAGES,) + KV
    return pl.pallas_call(
        patch_kernel,
        out_shape=jax.ShapeDtypeStruct(shape, BF16),
        in_specs=[VMEM] * 5,
        out_specs=HBM,
        scratch_shapes=[
            pltpu.VMEM(shape, BF16),
            pltpu.VMEM((MIG, 2 * HDIM), jnp.int32),
            pltpu.SMEM((MIG, 2 * HDIM), jnp.int32),
            pltpu.VMEM((MIG, 2 * HDIM), F32),
            DMA,
            DMA((MIG,)),
        ],
        compiler_params=pltpu.CompilerParams(vmem_limit_bytes=8 << 20),
        name="patch",
    )(moved, *parts)


def after(value, *others):
    return lax.optimization_barrier((value,) + others)[0]


def local(
    query_rows, new_kv, residual, kv_cache, page_table, lengths, migrate_ids,
    projection, kv_weight, norm_gain,
):
    replicas = lax.axis_size("inst")
    table = page_table.T

    def across(value, by):
        return lax.ppermute(value, "tensor", [(i, (i + 2 * by) % 8) for i in range(8)])

    def to_twin(value):
        return lax.ppermute(value, "tensor", [(i, i ^ 1) for i in range(8)])

    down = [(i, i // 4 * 4 + (i + 3) % 4) for i in range(replicas)]
    turn = [(i, (i + 3) % replicas) if i % 4 == 1 else pair for i, pair in enumerate(down)]

    def to_next(value):
        return lax.ppermute(
            value, "inst", [(i, (i + 1) % replicas) for i in range(replicas)]
        )

    pool = kv_cache[0]
    back, ahead, later = gather_pages(table, lengths, migrate_ids, new_kv, pool)
    ahead = to_next(ahead)
    back = lax.ppermute(back, "inst", down)

    attn, keep, give, weight = first_layer(
        table, lengths, query_rows, new_kv, pool, projection[0]
    )
    own, a, b, c = pair_sum(keep, to_twin(give), residual)
    share = share_sum(own, across(a, 1), across(b, 2), across(c, 3))
    across_z = [(2 * i, 2 * i + 1) for i in range(replicas)]
    across_z += [(b, a) for a, b in across_z if a % 8 != 6]
    arrived = lax.ppermute(share, ("inst", "section"), across_z)
    back = lax.ppermute(after(back, share), "inst", down)
    flat_kv = after(kv_weight, share).reshape(D, 2 * HDIM)
    steps = [
        (2 * i + k, 2 * ((i + 1) % replicas) + k) for i in range(replicas) for k in range(2)
    ]
    turns = [(a, b) for a, b in steps if a % 8 == 6]
    later = after(later, share)
    soon = lax.ppermute(later, ("inst", "section"), [p for p in steps if p not in turns])
    late = lax.ppermute(after(later, arrived), ("inst", "section"), turns)
    arrived = after(arrived, flat_kv, ahead)

    mine = [arrived] + [across(arrived, k) for k in (1, 2, 3)]
    other = [to_twin(after(arrived, mine[1]))] + [to_twin(m) for m in mine[1:]]
    back = lax.ppermute(after(back, *mine), "inst", turn)
    hidden, query, fresh, moved = project(
        migrate_ids, lengths, share, mine, other, norm_gain, weight, flat_kv
    )
    moved = lax.ppermute(
        moved,
        ("inst", "section"),
        [(2 * i + 1, 2 * ((i + 1) % replicas) + 1) for i in range(replicas)],
    )
    attn = second_layer(table, lengths, attn, query, fresh, pool)
    migrated = patch(moved, back, ahead, soon, late)
    return attn[None], hidden, migrated.reshape((1, MIG, PAGES) + KV)


def solution(mesh):
    return jax.shard_map(
        local,
        mesh=mesh,
        in_specs=(
            P("inst", "tensor"),
            P("inst", None, "tensor"),
            P("inst", "tensor"),
            P("section", "inst", None, None, "tensor"),
            P("inst", None),
            P("inst"),
            P("inst"),
            P("section", None, "tensor"),
            P(None, None, "tensor"),
            P(),
        ),
        out_specs=(
            P("section", "inst", "tensor"),
            P("inst", "tensor"),
            P("section", "inst", None, None, None, "tensor"),
        ),
        check_vma=False,
    )
```

```python
import functools

import jax
import jax.numpy as jnp
from jax import lax
from jax.experimental import pallas as pl
from jax.experimental.pallas import tpu as pltpu
from jax.sharding import PartitionSpec as P

HDIM = 128
PAGE = 128
PAGES = 4
REQ = 32
MIG = 8
HEADS = 4
SPAN = PAGES * PAGE
WIDTH = HEADS * HDIM
D = 4096
POOL = 128
SENT = 2 * MIG
GROUP = 16
PAD = 8
PARTS = (6, 15, 11)
SCALE = HDIM ** (-0.5)
F32 = jnp.float32
BF16 = jnp.bfloat16
HBM = pl.BlockSpec(memory_space=pltpu.HBM)
VMEM = pl.BlockSpec(memory_space=pltpu.VMEM)
DMA = pltpu.SemaphoreType.DMA
KV = (2, PAGE, HDIM)


def in_hbm(*values):
    return [pltpu.with_memory_space_constraint(v, pltpu.HBM) for v in values]


def in_vmem(*values):
    return [pltpu.with_memory_space_constraint(v, pltpu.VMEM) for v in values]


def leading():
    return lax.axis_index("section") == 0


def place():
    index = lax.axis_index("tensor")
    return index // 2, index % 2


def started(*copies):
    made = [pltpu.make_async_copy(*c) for c in copies]
    for c in made:
        c.start()
    return made


def scores(lengths, table, qs, ks, pages, ss, g):
    lane = lax.broadcasted_iota(jnp.int32, (PAD, SPAN), 1)
    rows = slice(g * GROUP * PAD, (g + 1) * GROUP * PAD)
    q = qs[rows, :]
    for i in range(GROUP):
        r = g * GROUP + i
        own = q[i * PAD : (i + 1) * PAD].astype(BF16)
        s = jnp.concatenate(
            [
                lax.dot_general(
                    own,
                    pages[table[p, r], 0],
                    (((1,), (1,)), ((), ())),
                    preferred_element_type=F32,
                )
                for p in range(PAGES)
            ],
            axis=1,
        )
        ss[r * PAD : (r + 1) * PAD, :] = jnp.where(
            lane < lengths[r] - 1, s * SCALE, F32(-1e30)
        )


def mix(table, qs, ks, vs, os, pages, ss, g):
    rows = slice(g * GROUP * PAD, (g + 1) * GROUP * PAD)
    fresh = jnp.sum(qs[rows, :] * ks[rows, :], axis=-1, keepdims=True) * SCALE
    s = ss[rows, :]
    top = jnp.maximum(jnp.max(s, axis=-1, keepdims=True), fresh)
    w = jnp.exp(s - top)
    fw = jnp.exp(fresh - top)
    total = jnp.sum(w, axis=-1, keepdims=True) + fw
    outs = []
    for i in range(GROUP):
        r = g * GROUP + i
        rounded = w[i * PAD : (i + 1) * PAD].astype(BF16)
        values = jnp.concatenate([pages[table[p, r], 1] for p in range(PAGES)], axis=0)
        outs.append(jnp.dot(rounded, values, preferred_element_type=F32))
    o = jnp.concatenate(outs, axis=0) + fw.astype(BF16).astype(F32) * vs[rows, :]
    os[rows, :] = o / total


def spread(qs, ks, vs, q, k, v):
    for dst in (qs, ks, vs):
        dst[...] = jnp.zeros_like(dst)
    for h in range(HEADS):
        at = pl.ds(h, REQ, stride=PAD)
        qs[at, :] = q[:, h * HDIM : (h + 1) * HDIM]
        ks[at, :] = k
        vs[at, :] = v


def collect(os, out):
    for h in range(HEADS):
        out[:, h * HDIM : (h + 1) * HDIM] = os[pl.ds(h, REQ, stride=PAD), :].astype(BF16)


ROW_SCRATCH = [pltpu.VMEM((REQ * PAD, HDIM), F32)] * 4 + [pltpu.VMEM((REQ * PAD, SPAN), F32)]
TABLE_SCRATCH = [pltpu.SMEM((PAGES, REQ), jnp.int32), pltpu.SMEM((REQ,), jnp.int32)]


def write_row(ref, index, row, key, value):
    base = pl.multiple_of(row // 16 * 16, 16)
    hit = lax.broadcasted_iota(jnp.int32, (16, HDIM), 0) == row - base
    for c, new in ((0, key), (1, value)):
        old = ref[index, c, pl.ds(base, 16), :].astype(F32)
        ref[index, c, pl.ds(base, 16), :] = jnp.where(hit, new, old).astype(BF16)


def page_slots(refs):
    return [(ref, i) for ref, count in zip(refs, PARTS) for i in range(count)]


def gather_kernel(
    table_in, lengths_in, ids_in, fresh_in, pool, back, ahead, later,
    table, lengths, ids, fresh, small, sems,
):
    small_copies = started(
        (table_in, table, small.at[0]),
        (lengths_in, lengths, small.at[1]),
        (ids_in, ids, small.at[2]),
        (fresh_in, fresh, small.at[3]),
    )
    for c in small_copies[:3]:
        c.wait()
    slots = page_slots((back, ahead, later))

    def each(act):
        for j in range(MIG):
            r = ids[j]
            for p in range(PAGES):
                ref, index = slots[j * PAGES + p]
                act(r, p, ref.at[index], sems.at[j * PAGES + p])

    def start(r, p, slot, sem):
        used = p * PAGE < lengths[r]

        @pl.when(used)
        def _():
            pltpu.make_async_copy(pool.at[table[p, r]], slot, sem).start()

        @pl.when(jnp.logical_not(used))
        def _():
            slot[...] = jnp.zeros(KV, BF16)

    def wait(r, p, slot, sem):
        @pl.when(p * PAGE < lengths[r])
        def _():
            pltpu.make_async_copy(pool.at[0], slot, sem).wait()

    each(start)
    small_copies[3].wait()
    each(wait)

    @pl.when(leading())
    def _():
        for j in range(MIG):
            r = ids[j]
            last = lengths[r] - 1
            row = fresh[r].astype(F32)
            for p in range(PAGES):
                ref, index = slots[j * PAGES + p]

                @pl.when(last // PAGE == p)
                def _():
                    write_row(ref, index, last % PAGE, row[0:1], row[1:2])


def gather_pages(table, lengths, ids, fresh, pool):
    return pl.pallas_call(
        gather_kernel,
        out_shape=[jax.ShapeDtypeStruct((count,) + KV, BF16) for count in PARTS],
        in_specs=[HBM] * 5,
        out_specs=[VMEM] * 3,
        scratch_shapes=TABLE_SCRATCH
        + [
            pltpu.SMEM((MIG,), jnp.int32),
            pltpu.VMEM((REQ, 2, HDIM), BF16),
            DMA((4,)),
            DMA((MIG * PAGES,)),
        ],
        compiler_params=pltpu.CompilerParams(vmem_limit_bytes=4 << 20),
        name="gather_pages",
    )(*in_hbm(table, lengths, ids, fresh, pool))


def first_kernel(
    table_in, lengths_in, query_in, fresh_in, pages, weight_in,
    attn, keep, give, weight,
    qs, ks, vs, os, ss, table, lengths, query, fresh, small, wsem,
):
    y, core = place()
    lead = leading()
    [weight_copy] = started((weight_in, weight, wsem))

    @pl.when(lead)
    def _():
        copies = started(
            (table_in, table, small.at[0]),
            (lengths_in, lengths, small.at[1]),
            (query_in, query, small.at[2]),
            (fresh_in, fresh, small.at[3]),
        )
        for c in copies:
            c.wait()
        spread(
            qs, ks, vs,
            query[...].astype(F32), fresh[:, 0, :].astype(F32), fresh[:, 1, :].astype(F32),
        )
        for g in range(REQ // GROUP):
            scores(lengths, table, qs, ks, pages, ss, g)
        for g in range(REQ // GROUP):
            mix(table, qs, ks, vs, os, pages, ss, g)
        collect(os, attn)

    weight_copy.wait()

    @pl.when(lead)
    def _():
        a = attn[...]
        for out, c in ((give, 1 - core), (keep, core)):
            for k in range(4):
                block = lax.rem(y + k, 4) * 2 + c
                w = weight[pl.ds(pl.multiple_of(block * WIDTH, WIDTH), WIDTH), :]
                out[k] = lax.dot_general(
                    a, w, (((1,), (1,)), ((), ())), preferred_element_type=F32
                )

    @pl.when(jnp.logical_not(lead))
    def _():
        attn[...] = jnp.zeros_like(attn)
        keep[...] = jnp.zeros_like(keep)
        give[...] = jnp.zeros_like(give)


def first_layer(table, lengths, query, fresh, pages, weight):
    part = (4, REQ, WIDTH)
    return pl.pallas_call(
        first_kernel,
        out_shape=(
            jax.ShapeDtypeStruct((REQ, WIDTH), BF16),
            jax.ShapeDtypeStruct(part, F32),
            jax.ShapeDtypeStruct(part, F32),
            pltpu.VMEM((D, WIDTH), BF16),
        ),
        in_specs=[HBM] * 4 + [VMEM, HBM],
        out_specs=(VMEM,) * 4,
        scratch_shapes=ROW_SCRATCH
        + TABLE_SCRATCH
        + [
            pltpu.VMEM((REQ, WIDTH), BF16),
            pltpu.VMEM((REQ, 2, HDIM), BF16),
            DMA((4,)),
            DMA,
        ],
        compiler_params=pltpu.CompilerParams(vmem_limit_bytes=8 << 20),
        name="first_layer",
    )(*in_hbm(table, lengths, query, fresh), *in_vmem(pages), *in_hbm(weight))


def pair_kernel(keep, got, residual, own, a, b, c):
    own[...] = keep[0] + got[0] + residual[...].astype(F32)
    for k, out in ((1, a), (2, b), (3, c)):
        out[...] = (keep[k] + got[k]).astype(BF16)


def pair_sum(keep, got, residual):
    share = (REQ, WIDTH)
    return pl.pallas_call(
        pair_kernel,
        out_shape=(jax.ShapeDtypeStruct(share, F32),)
        + (jax.ShapeDtypeStruct(share, BF16),) * 3,
        in_specs=[VMEM] * 3,
        out_specs=(VMEM,) * 4,
        compiler_params=pltpu.CompilerParams(vmem_limit_bytes=4 << 20),
        name="pair_sum",
    )(keep, got, residual)


def share_kernel(own, a, b, c, share):
    total = own[...] + a[...].astype(F32) + b[...].astype(F32) + c[...].astype(F32)
    share[...] = total.astype(BF16)


def share_sum(own, a, b, c):
    return pl.pallas_call(
        share_kernel,
        out_shape=jax.ShapeDtypeStruct((REQ, WIDTH), BF16),
        in_specs=[VMEM] * 4,
        out_specs=VMEM,
        compiler_params=pltpu.CompilerParams(vmem_limit_bytes=4 << 20),
        name="share_sum",
    )(own, a, b, c)


def project_kernel(
    ids_in, lengths_in, share, m0, m1, m2, m3, n0, n1, n2, n3, gain, weight, kv_weight,
    hidden, query, fresh, moved,
    sent, ids, lengths, small,
):
    y, core = place()
    lead = leading()

    @pl.when(lead)
    def _():
        hidden[...] = share[...]
        query[...] = jnp.zeros_like(query)
        fresh[...] = jnp.zeros_like(fresh)
        moved[...] = jnp.zeros_like(moved)

    @pl.when(jnp.logical_not(lead))
    def _():
        copies = started((ids_in, ids, small.at[0]), (lengths_in, lengths, small.at[1]))
        hidden[...] = m0[...]
        blocks = []
        square = jnp.zeros((REQ, 1), F32)
        for refs, c in (((m0, m1, m2, m3), core), ((n0, n1, n2, n3), 1 - core)):
            for k, ref in enumerate(refs):
                x = ref[...].astype(F32)
                square += jnp.sum(x * x, axis=-1, keepdims=True)
                blocks.append((x, lax.rem(y + 4 - k, 4) * 2 + c))
        factor = lax.rsqrt(square * (1.0 / D) + 1e-05)
        q = jnp.zeros((REQ, WIDTH), F32)
        kv = jnp.zeros((REQ, 2 * HDIM), F32)
        for x, block in blocks:
            at = pl.ds(pl.multiple_of(block * WIDTH, WIDTH), WIDTH)
            x = (x * factor * gain[at].reshape(1, WIDTH)).astype(BF16)
            q += jnp.dot(x, weight[at, :], preferred_element_type=F32)
            kv += jnp.dot(x, kv_weight[at, :], preferred_element_type=F32)
        query[...] = q.astype(BF16)
        fresh[...] = kv.astype(BF16).astype(F32)
        for copy in copies:
            copy.wait()
        lane = lax.broadcasted_iota(jnp.int32, (1, 2 * HDIM), 1)
        for j in range(MIG):
            r = ids[j]
            sent[pl.ds(j, 1), :] = fresh[pl.ds(r, 1), :]
            last = lengths[r] - 1
            sent[pl.ds(MIG + j, 1), :] = jnp.where(
                lane < HDIM, last // PAGE, last % PAGE
            ).astype(F32)
        moved[...] = sent[...].astype(BF16)


def project(ids, lengths, share, mine, other, gain, weight, kv_weight):
    return pl.pallas_call(
        project_kernel,
        out_shape=(
            jax.ShapeDtypeStruct((REQ, WIDTH), BF16),
            jax.ShapeDtypeStruct((REQ, WIDTH), BF16),
            jax.ShapeDtypeStruct((REQ, 2 * HDIM), F32),
            jax.ShapeDtypeStruct((SENT, 2 * HDIM), BF16),
        ),
        in_specs=[HBM] * 2 + [VMEM] * 12,
        out_specs=(VMEM,) * 4,
        scratch_shapes=[
            pltpu.VMEM((SENT, 2 * HDIM), F32),
            pltpu.SMEM((MIG,), jnp.int32),
            pltpu.SMEM((REQ,), jnp.int32),
            DMA((2,)),
        ],
        compiler_params=pltpu.CompilerParams(vmem_limit_bytes=8 << 20),
        name="project",
    )(*in_hbm(ids, lengths), share, *mine, *other, gain, *in_vmem(weight, kv_weight))


def second_kernel(
    table_in, lengths_in, first_attn, query, fresh, pages, attn,
    qs, ks, vs, os, ss, table, lengths, small,
):
    @pl.when(jnp.logical_not(leading()))
    def _():
        copies = started((table_in, table, small.at[0]), (lengths_in, lengths, small.at[1]))
        spread(qs, ks, vs, query[...].astype(F32), fresh[:, :HDIM], fresh[:, HDIM:])
        for copy in copies:
            copy.wait()
        for g in range(REQ // GROUP):
            scores(lengths, table, qs, ks, pages, ss, g)
        for g in range(REQ // GROUP):
            mix(table, qs, ks, vs, os, pages, ss, g)
        collect(os, attn)

    @pl.when(leading())
    def _():
        attn[...] = first_attn[...]


def second_layer(table, lengths, first_attn, query, fresh, pages):
    return pl.pallas_call(
        second_kernel,
        out_shape=jax.ShapeDtypeStruct((REQ, WIDTH), BF16),
        in_specs=[HBM] * 2 + [VMEM] * 4,
        out_specs=VMEM,
        scratch_shapes=ROW_SCRATCH + TABLE_SCRATCH + [DMA((2,))],
        compiler_params=pltpu.CompilerParams(vmem_limit_bytes=8 << 20),
        cost_estimate=pl.CostEstimate(
            flops=1 << 30, bytes_accessed=16 << 20, transcendentals=1 << 20
        ),
        name="second_layer",
    )(*in_hbm(table, lengths), first_attn, query, fresh, *in_vmem(pages))


def patch_kernel(moved, back, ahead, soon, late, out, held, whole, last, rows, small, outsem):
    whole[...] = moved[MIG:, :].astype(F32).astype(jnp.int32)
    rows[...] = moved[:MIG, :].astype(F32)
    [last_copy] = started((whole, last, small))
    for i, (ref, index) in enumerate(page_slots((back, ahead))):
        held[i] = ref[index]
    turned = jnp.logical_and(leading(), lax.rem(lax.axis_index("inst"), 4) == 0)
    first = PARTS[0] + PARTS[1]

    @pl.when(turned)
    def _():
        for i in range(PARTS[2]):
            held[first + i] = late[i]

    @pl.when(jnp.logical_not(turned))
    def _():
        for i in range(PARTS[2]):
            held[first + i] = soon[i]

    last_copy.wait()
    lead = leading()
    leave = []
    for j in range(MIG):

        @pl.when(jnp.logical_not(lead))
        def _():
            write_row(
                held,
                j * PAGES + last[j, 0],
                last[j, HDIM],
                rows[pl.ds(j, 1), :HDIM],
                rows[pl.ds(j, 1), HDIM:],
            )

        at = pl.ds(j * PAGES, PAGES)
        leave += started((held.at[at], out.at[at], outsem.at[j]))
    for c in leave:
        c.wait()


def patch(moved, *parts):
    shape = (MIG * PAGES,) + KV
    return pl.pallas_call(
        patch_kernel,
        out_shape=jax.ShapeDtypeStruct(shape, BF16),
        in_specs=[VMEM] * 5,
        out_specs=HBM,
        scratch_shapes=[
            pltpu.VMEM(shape, BF16),
            pltpu.VMEM((MIG, 2 * HDIM), jnp.int32),
            pltpu.SMEM((MIG, 2 * HDIM), jnp.int32),
            pltpu.VMEM((MIG, 2 * HDIM), F32),
            DMA,
            DMA((MIG,)),
        ],
        compiler_params=pltpu.CompilerParams(vmem_limit_bytes=8 << 20),
        name="patch",
    )(moved, *parts)


def after(value, *others):
    return lax.optimization_barrier((value,) + others)[0]


def local(
    query_rows, new_kv, residual, kv_cache, page_table, lengths, migrate_ids,
    projection, kv_weight, norm_gain,
):
    replicas = lax.axis_size("inst")
    table = page_table.T

    def across(value, by):
        return lax.ppermute(value, "tensor", [(i, (i + 2 * by) % 8) for i in range(8)])

    def to_twin(value):
        return lax.ppermute(value, "tensor", [(i, i ^ 1) for i in range(8)])

    down = [(i, i // 4 * 4 + (i + 3) % 4) for i in range(replicas)]
    turn = [(i, (i + 3) % replicas) if i % 4 == 1 else pair for i, pair in enumerate(down)]

    def to_next(value):
        return lax.ppermute(
            value, "inst", [(i, (i + 1) % replicas) for i in range(replicas)]
        )

    pool = kv_cache[0]
    back, ahead, later = gather_pages(table, lengths, migrate_ids, new_kv, pool)
    ahead = to_next(ahead)
    back = lax.ppermute(back, "inst", down)

    attn, keep, give, weight = first_layer(
        table, lengths, query_rows, new_kv, pool, projection[0]
    )
    own, a, b, c = pair_sum(keep, to_twin(give), residual)
    share = share_sum(own, across(a, 1), across(b, 2), across(c, 3))
    across_z = [(2 * i, 2 * i + 1) for i in range(replicas)]
    across_z += [(b, a) for a, b in across_z if a % 8 != 6]
    arrived = lax.ppermute(share, ("inst", "section"), across_z)
    back = lax.ppermute(after(back, share), "inst", down)
    flat_kv = after(kv_weight, share).reshape(D, 2 * HDIM)
    steps = [
        (2 * i + k, 2 * ((i + 1) % replicas) + k) for i in range(replicas) for k in range(2)
    ]
    turns = [(a, b) for a, b in steps if a % 8 == 6]
    later = after(later, share)
    soon = lax.ppermute(later, ("inst", "section"), [p for p in steps if p not in turns])
    late = lax.ppermute(after(later, arrived), ("inst", "section"), turns)
    arrived = after(arrived, flat_kv, ahead)

    mine = [arrived] + [across(arrived, k) for k in (1, 2, 3)]
    other = [to_twin(after(arrived, mine[1]))] + [to_twin(m) for m in mine[1:]]
    back = lax.ppermute(after(back, *mine), "inst", turn)
    hidden, query, fresh, moved = project(
        migrate_ids, lengths, share, mine, other, norm_gain, weight, flat_kv
    )
    moved = lax.ppermute(
        moved,
        ("inst", "section"),
        [(2 * i + 1, 2 * ((i + 1) % replicas) + 1) for i in range(replicas)],
    )
    attn = second_layer(table, lengths, attn, query, fresh, pool)
    migrated = patch(moved, back, ahead, soon, late)
    return attn[None], hidden, migrated.reshape((1, MIG, PAGES) + KV)


def solution(mesh):
    return jax.shard_map(
        local,
        mesh=mesh,
        in_specs=(
            P("inst", "tensor"),
            P("inst", None, "tensor"),
            P("inst", "tensor"),
            P("section", "inst", None, None, "tensor"),
            P("inst", None),
            P("inst"),
            P("inst"),
            P("section", None, "tensor"),
            P(None, None, "tensor"),
            P(),
        ),
        out_specs=(
            P("section", "inst", "tensor"),
            P("inst", "tensor"),
            P("section", "inst", None, None, None, "tensor"),
        ),
        check_vma=False,
    )
```
